128 devices in a mesh: tm: 8 (over z, x_hi), docs: 16 (over y, x_lo, core).
Axes of the slice: x: 4 (x_hi: 2, x_lo: 2; x = x_hi * 2 + x_lo), y: 4, z: 4, core: 2. Of those that a mesh axis runs over, the one named last changes fastest.
Arguments:
- counts: int32 [8, 1024, 32768], P('tm', 'docs'), may hold values from 0 to 5, as said below
- topic_means: float32 [8, 32768, 128], P('tm', 'docs'), may hold values from -80 to 170
- doc_topics_init: float32 [8, 1024, 128], P('tm', 'docs'), may hold values from 0.5 to 20
- dirichlet_prior: float32 [128], replicated, may hold values from 0.05 to 1
- chain_var: float32 [128], replicated, may hold values from 0.005 to 0.5
- obs_noise: float32 [128], replicated, may hold values from 0.1 to 10
Outputs:
- smoothed_means: float32 [8, 32768, 128], P('tm', 'docs')
- doc_topics: float32 [8, 1024, 128], P('tm', 'docs')
The draws below stay inside these ranges and needn't reach their ends.
Inputs may be any that keep to these rules, and one draw needn't show every extreme that they name: `counts`: each entry is 0 or a count of 1 to 5; each word has its own share of nonzero entries, between a quarter and three quarters.
All inputs are finite; a program needn't handle non-finite values.
Results may differ from the reference program's by a relative error of at most 0.01.
Values may be sent and summed in bfloat16 or wider, within the bound.
No kernel may reach another device: no remote copies, remote signals or barrier semaphores. Data moves between devices by JAX's collectives and lax.ppermute only.
A program may use at most 128 MiB of HBM per device.

```python
import math
import jax
import jax.numpy as jnp
from jax import lax

V = 32768
K = 128
ITERS_E = 4
SLICES = 8
DOCS_ALL = 1024


def draw_counts(key, part):
    chance_key, value_key, density_key = jax.random.split(key, 3)
    density = jax.random.randint(density_key, (V,), 16, 49)
    chance = jax.random.randint(chance_key, (SLICES, DOCS_ALL, V), 0, 64)
    values = jax.random.randint(value_key, (SLICES, DOCS_ALL, V), 1, 6)
    return jnp.where(chance < density[None, None, :], values, 0).astype(jnp.int32)


def draw_topic_means(key, part):
    streams = jax.random.split(key, 2)
    rough_part = 1.5 * jnp.clip(jax.random.normal(streams[0], (SLICES, V, K), jnp.float32), -4.0, 4.0)
    offset = jax.random.uniform(streams[1], (SLICES, 1, K), jnp.float32, -2.0, 2.0)
    return (rough_part + offset).astype(jnp.float32)


def steps_of(stream_key, extent, cuts, smallest, top_value):
    level, own = 1.0, jax.random.fold_in(stream_key, 6)
    for position, parts in cuts:
        heights = jnp.exp(jax.random.uniform(jax.random.fold_in(own, position), (parts,), jnp.float32, smallest / len(cuts), top_value / len(cuts)))
        level = level * jnp.repeat(heights, extent[position] // parts).reshape([-1 if axis == position else 1 for axis in range(len(extent))])
    return level


def setup_inputs(seed: int = 0) -> dict:
    seeds = jax.random.split(jax.random.key(seed), 7)
    counts = draw_counts(jax.random.fold_in(seeds[6], 71), 0)
    topic_means = draw_topic_means(jax.random.fold_in(seeds[6], 71), 0)
    doc_topics_init = jnp.clip(jnp.exp(math.log(20.0) - 3.6888795 * jax.random.uniform(seeds[2], (SLICES, DOCS_ALL, K), jnp.float32) ** steps_of(seeds[2], (SLICES, DOCS_ALL, K), ((0, 8), (1, 16)), -0.2, 0.2)), 0.5, 20.0)
    dirichlet_prior = jnp.clip(jnp.exp(jax.random.uniform(seeds[3], (K,), jnp.float32, math.log(0.05), math.log(1.0))), 0.05, 1.0)
    chain_var = jnp.clip(jnp.exp(jax.random.uniform(seeds[4], (K,), jnp.float32, math.log(0.005), math.log(0.5))), 0.005, 0.5)
    obs_noise = jnp.clip(jnp.exp(jax.random.uniform(seeds[5], (K,), jnp.float32, math.log(0.1), math.log(10.0))), 0.1, 10.0)
    return dict(counts=counts, topic_means=topic_means, doc_topics_init=doc_topics_init, dirichlet_prior=dirichlet_prior, chain_var=chain_var, obs_noise=obs_noise)


prior_count = 0.5
initial_scale = 1000.0


def chain_factors(totals, chain_var, obs_noise):
    relative = jnp.sum(totals, axis=1, keepdims=True) / (totals.shape[1] * totals)
    noise = obs_noise[None, :] * relative

    def advance(previous, noise_level):
        predicted = previous + chain_var
        own_gain = predicted / (predicted + noise_level)
        current = (1.0 - own_gain) * predicted
        return current, (own_gain, current)

    unused, (gains, filtered_var) = lax.scan(advance, initial_scale * chain_var, noise)
    smooth = filtered_var / (filtered_var + chain_var)
    smooth = jnp.concatenate([smooth[:-1], jnp.zeros_like(smooth[-1:])], axis=0)
    return gains, smooth


def reference(counts, topic_means, doc_topics_init, dirichlet_prior, chain_var, obs_noise):
    def one_slice(inputs):
        count_rows, slab_means, concentration = inputs
        beta = jax.nn.softmax(slab_means, axis=0).astype(jnp.bfloat16)
        beta_wide = beta.astype(jnp.float32)
        count_wide = count_rows.astype(jnp.float32)
        for sweep_index in range(ITERS_E):
            proportions = jnp.exp(lax.digamma(concentration)).astype(jnp.bfloat16)
            theta_wide = proportions.astype(jnp.float32)
            mixture = jnp.dot(theta_wide, beta_wide.T, preferred_element_type=jnp.float32)
            ratios = (count_wide / mixture).astype(jnp.bfloat16)
            ratio_wide = ratios.astype(jnp.float32)
            update = theta_wide * jnp.dot(ratio_wide, beta_wide, preferred_element_type=jnp.float32)
            concentration = dirichlet_prior[None, :] + update
        word_stats = beta_wide * jnp.dot(ratio_wide.T, theta_wide, preferred_element_type=jnp.float32)
        return word_stats, concentration, jnp.sum(update, axis=0)

    word_stats, doc_topics, totals = lax.map(one_slice, (counts, topic_means, doc_topics_init))
    gains, smooth = chain_factors(totals, chain_var, obs_noise)
    pseudo = jnp.log(word_stats + prior_count) - jnp.log((totals[:, None, :] + prior_count * V) / V)

    def forward(previous, inputs):
        own_gain, observed = inputs
        current = (1.0 - own_gain) * previous + own_gain * observed
        return current, current

    unused, filtered = lax.scan(forward, jnp.zeros_like(pseudo[0]), (gains[:, None, :], pseudo))

    def backward(following, inputs):
        factor, current = inputs
        result = (1.0 - factor) * current + factor * following
        return result, result

    unused, smoothed = lax.scan(backward, jnp.zeros_like(pseudo[0]), (smooth[:, None, :], filtered), reverse=True)
    return smoothed, doc_topics
```

```python
import functools

import jax
import jax.numpy as jnp
from jax import lax
from jax.experimental import pallas as pl
from jax.experimental.pallas import tpu as pltpu
from jax.sharding import Mesh
from jax.sharding import PartitionSpec as P


V = 32768
K = 128
SLAB = 2048
HALF = 1024
DOCS = 64
TILE = 512
ITERS_E = 4
TM = ("z", "xh")

prior_count = 0.5
initial_scale = 1000.0

F32 = jnp.float32
BF16 = jnp.bfloat16

REL = [(dy, dx) for dy in range(4) for dx in range(2)]


def across(x):
    return lax.ppermute(x, "c", [(0, 1), (1, 0)])


def xswap(x):
    return lax.ppermute(x, "xl", [(0, 1), (1, 0)])


def yfrom(x, dy):
    return lax.ppermute(x, "y", [((i + dy) % 4, i) for i in range(4)])


def hbm(n):
    return [pl.BlockSpec(memory_space=pl.ANY)] * n


def vmem(n):
    return [pl.BlockSpec(memory_space=pltpu.VMEM)] * n


def split3(x):
    hi = x.astype(BF16)
    rest = x - hi.astype(F32)
    mid = rest.astype(BF16)
    low = (rest - mid.astype(F32)).astype(BF16)
    return hi, mid, low


def slab_kernel(x_ref, b0_ref, b1_ref, l_ref, e_ref):
    def peak(i, m):
        return jnp.maximum(m, jnp.max(x_ref[pl.ds(i * 256, 256), :].reshape(32, 8, K), axis=0))

    m8 = lax.fori_loop(0, 8, peak, jnp.full((8, K), -jnp.inf, F32))
    m = jnp.max(m8, axis=0, keepdims=True)

    def mass(i, s):
        e = jnp.exp(x_ref[pl.ds(i * 256, 256), :] - m)
        e_ref[pl.ds(i * 256, 256), :] = e
        return s + jnp.sum(e.reshape(32, 8, K), axis=0)

    s8 = lax.fori_loop(0, 8, mass, jnp.zeros((8, K), F32))
    s = jnp.sum(s8, axis=0, keepdims=True)
    inverse = 1.0 / s
    l_ref[...] = jnp.broadcast_to(m + jnp.log(s), (8, K))
    for h, out in enumerate((b0_ref, b1_ref)):

        @pl.loop(0, 4)
        def _(i, h=h, out=out):
            out[pl.ds(i * 256, 256), :] = (
                e_ref[pl.ds(h * HALF + i * 256, 256), :] * inverse
            ).astype(BF16)


def slab_softmax(x):
    return pl.pallas_call(
        slab_kernel,
        out_shape=(
            jax.ShapeDtypeStruct((HALF, K), BF16),
            jax.ShapeDtypeStruct((HALF, K), BF16),
            jax.ShapeDtypeStruct((8, K), F32),
        ),
        in_specs=vmem(1),
        out_specs=tuple(vmem(3)),
        scratch_shapes=[pltpu.VMEM((SLAB, K), F32)],
        name="slab_softmax",
    )(x)


def counts_kernel(own_at, give_at, own_ref, give_ref, own_out, give_out):
    own_out[0] = own_ref[...].astype(F32).astype(BF16)
    give_out[0] = give_ref[...].astype(F32).astype(BF16)


def split_counts(counts, own_at, give_at):
    spec = pltpu.PrefetchScalarGridSpec(
        num_scalar_prefetch=2,
        grid=(8,),
        in_specs=[
            pl.BlockSpec((DOCS, SLAB), lambda r, o, g: (0, o[r])),
            pl.BlockSpec((DOCS, SLAB), lambda r, o, g: (0, g[r])),
        ],
        out_specs=[pl.BlockSpec((1, DOCS, SLAB), lambda r, o, g: (r, 0, 0))] * 2,
    )
    return pl.pallas_call(
        counts_kernel,
        grid_spec=spec,
        out_shape=[jax.ShapeDtypeStruct((8, DOCS, SLAB), BF16)] * 2,
        cost_estimate=pl.CostEstimate(flops=0, bytes_accessed=12 << 20, transcendentals=0),
        name="split_counts",
    )(own_at, give_at, counts, counts)


def digamma(x):
    total = jnp.zeros_like(x)
    for i in range(8):
        total = total + 1.0 / (x + float(i))
    y = x + 8.0
    r = 1.0 / y
    r2 = r * r
    tail = r2 * (1.0 / 12.0 - r2 * (1.0 / 120.0 - r2 * (1.0 / 252.0 - r2 * (1.0 / 240.0))))
    return jnp.log(y) - 0.5 * r - tail - total


def sweep_kernel(first, slabs, stats, *refs):
    n = len(slabs)
    refs = list(refs)
    if first == "init":
        own0, other0 = refs[:2]
        refs = refs[2:]
    elif first == "parts":
        part0, part1, before, prior = refs[:4]
        refs = refs[4:]
    else:
        given = refs[0]
        refs = refs[1:]
    scale, b_refs, mine, theirs = refs[0], refs[1 : 1 + 2 * n], refs[1 + 2 * n], refs[2 + 2 * n]
    refs = refs[3 + 2 * n :]
    if first != "given":
        p_out = refs.pop(0)
    part = refs.pop(0)
    if stats:
        stat_refs = refs[: 2 * n]
        refs = refs[2 * n :]
    bs, cs, ps, sem_b, sem_c = refs

    copies = []
    for i, r in enumerate(slabs):
        group = []
        for h in range(2):
            group.append(
                pltpu.make_async_copy(
                    b_refs[2 * i + h], bs.at[i, pl.ds(h * HALF, HALF)], sem_b.at[i, h]
                )
            )
        for side, ref in enumerate((mine, theirs)):
            group.append(
                pltpu.make_async_copy(
                    ref.at[r], cs.at[i, pl.ds(side * DOCS, DOCS)], sem_c.at[i, side]
                )
            )
        for copy in group:
            copy.start()
        copies.append(group)

    if first == "given":
        p = given[...]
    else:
        if first == "init":
            gamma = jnp.concatenate([own0[...], other0[...]], axis=0)
        else:
            got = part1[...]
            total = part0[...] + jnp.concatenate([got[DOCS:], got[:DOCS]], axis=0)
            gamma = prior[...] + before[...].astype(F32) * total
        p = jnp.exp(digamma(gamma)).astype(BF16)
        p_out[...] = p
    p32 = p.astype(F32)
    for i, r in enumerate(slabs):
        ps[i] = (p32 * scale[r : r + 1, :]).astype(BF16)
    if stats:
        pt = p32.T.astype(BF16)

    part[...] = jnp.zeros((2 * DOCS, K), F32)
    for i, r in enumerate(slabs):
        for copy in copies[i]:
            copy.wait()

        def tile(w, acc, i=i):
            at = pl.multiple_of(w * TILE, TILE)
            b = bs[i, pl.ds(at, TILE), :]
            mixture = lax.dot_general(
                ps[i], b, (((1,), (1,)), ((), ())), preferred_element_type=F32
            )
            ratio = (cs[i, :, pl.ds(at, TILE)].astype(F32) / mixture).astype(BF16)
            return ratio, acc + jnp.dot(ratio, b, preferred_element_type=F32)

        acc = jnp.zeros((2 * DOCS, K), F32)
        if stats:
            for h in range(2):

                def step(w, acc, i=i, h=h):
                    ratio, acc = tile(w + h * (HALF // TILE), acc, i)
                    at = pl.multiple_of(w * TILE, TILE)
                    stat_refs[2 * i + h][:, pl.ds(at, TILE)] = jnp.dot(
                        pt, ratio, preferred_element_type=F32
                    ).astype(BF16)
                    return acc

                acc = lax.fori_loop(0, HALF // TILE, step, acc, unroll=True)
        else:
            acc = lax.fori_loop(0, SLAB // TILE, lambda w, a: tile(w, a)[1], acc, unroll=True)
        part[...] += acc * scale[r : r + 1, :]


def sweep(first, heads, scale, beta, mine, theirs, slabs=tuple(range(8)), stats=False):
    n = len(slabs)
    outs = []
    if first != "given":
        outs.append(jax.ShapeDtypeStruct((2 * DOCS, K), BF16))
    outs.append(jax.ShapeDtypeStruct((2 * DOCS, K), F32))
    if stats:
        outs += [jax.ShapeDtypeStruct((K, HALF), BF16)] * (2 * n)
    pieces = [beta[REL[r] + (h,)] for r in slabs for h in range(2)]
    return pl.pallas_call(
        functools.partial(sweep_kernel, first, slabs, stats),
        out_shape=outs,
        in_specs=vmem(len(heads) + 1) + hbm(2 * n + 2),
        out_specs=vmem(len(outs)),
        scratch_shapes=[
            pltpu.VMEM((n, SLAB, K), BF16),
            pltpu.VMEM((n, 2 * DOCS, SLAB), BF16),
            pltpu.VMEM((n, 2 * DOCS, K), BF16),
            pltpu.SemaphoreType.DMA((n, 2)),
            pltpu.SemaphoreType.DMA((n, 2)),
        ],
        compiler_params=pltpu.CompilerParams(vmem_limit_bytes=32 << 20),
        cost_estimate=pl.CostEstimate(
            flops=(6 if stats else 4) * 2 * DOCS * K * SLAB * n,
            bytes_accessed=n << 20,
            transcendentals=2 * DOCS * SLAB * n,
        ),
        name="sweep_" + first + str(n),
    )(*heads, scale, *pieces, mine, theirs)


def gather(h0, h1):
    r = {(0, 0, 0): h0, (0, 0, 1): h1}
    r[0, 1, 0] = xswap(h0)
    r[3, 0, 0] = yfrom(h0, 3)
    r[1, 0, 1] = yfrom(h1, 1)
    r[0, 1, 1] = xswap(h1)
    r[3, 0, 1] = yfrom(h1, 3)
    r[1, 0, 0] = yfrom(h0, 1)
    r[3, 1, 0] = xswap(r[3, 0, 0])
    r[2, 0, 0] = yfrom(r[3, 0, 0], 3)
    r[2, 0, 1] = yfrom(r[1, 0, 1], 1)
    r[1, 1, 0] = xswap(r[1, 0, 0])
    r[3, 1, 1] = yfrom(r[0, 1, 1], 3)
    r[1, 1, 1] = yfrom(r[0, 1, 1], 1)
    r[2, 1, 0] = xswap(r[2, 0, 0])
    r[2, 1, 1] = yfrom(r[3, 1, 1], 3)
    return r


def plus(*terms):
    total = terms[0].astype(F32)
    for term in terms[1:]:
        total = total + term.astype(F32)
    return total.astype(BF16)


def scatter(s):
    down = lambda x: yfrom(x, 1)
    up = lambda x: yfrom(x, 3)
    x1 = xswap(s[2, 1, 0])
    u1 = down(s[2, 1, 1])
    x2 = xswap(s[1, 1, 0])
    d2 = up(s[1, 1, 1])
    u2 = down(plus(s[3, 1, 1], u1))
    x3 = xswap(s[3, 1, 0])
    d3 = up(s[2, 0, 1])
    u3 = down(plus(s[2, 0, 0], x1))
    u4 = down(s[3, 0, 1])
    x4 = xswap(plus(s[0, 1, 1], u2, d2))
    d4 = up(plus(s[1, 0, 0], x2))
    x5 = xswap(s[0, 1, 0])
    d5 = up(plus(s[1, 0, 1], d3))
    u5 = down(plus(s[3, 0, 0], x3, u3))
    return (s[0, 0, 0], x5, u5, d4), (s[0, 0, 1], x4, u4, d5)


def pseudo_kernel(*refs):
    halves = (refs[0:4], refs[4:8])
    x_ref, l_ref, total_ref, out = refs[8:12]
    total = total_ref[0:1, :]
    level = jnp.log((total + prior_count * V) / V)
    for h in range(2):
        for q in range(4):
            rows = slice(q * 256, (q + 1) * 256)
            acc = halves[h][0][:, rows].astype(F32)
            for ref in halves[h][1:]:
                acc = acc + ref[:, rows].astype(F32)
            x = x_ref[h * HALF + q * 256 : h * HALF + (q + 1) * 256, :]
            beta = jnp.exp(x - l_ref[0:1, :]).astype(BF16).astype(F32)
            out[4 * h + q, 0:256, :] = (jnp.log(beta * acc.T + prior_count) - level).astype(BF16)
    hi, mid, low = split3(total)
    row = lax.broadcasted_iota(jnp.int32, (16, K), 0)
    head = jnp.where(row == 0, hi.astype(F32), jnp.where(row == 1, mid.astype(F32), low.astype(F32)))
    for t in range(8):
        out[t, 256:272, :] = head.astype(BF16)


def pseudo_rows(half0, half1, x, level, total):
    return pl.pallas_call(
        pseudo_kernel,
        out_shape=jax.ShapeDtypeStruct((8, 272, K), BF16),
        in_specs=vmem(11),
        out_specs=pl.BlockSpec(memory_space=pltpu.VMEM),
        name="pseudo_rows",
    )(*half0, *half1, x, level, total)


def smooth_kernel(y_ref, var_ref, noise_ref, out):
    var = var_ref[...]
    gains, factors = [], []
    previous = initial_scale * var
    for t in range(8):
        head = y_ref[t, 256:272, :].astype(F32)
        total = head[0:1] + head[1:2] + head[2:3]
        noise = noise_ref[...] * jnp.sum(total, axis=1, keepdims=True) / (K * total)
        predicted = previous + var
        gain = predicted / (predicted + noise)
        previous = (1.0 - gain) * predicted
        gains.append(gain)
        factors.append(previous / (previous + var))

    @pl.loop(0, 8)
    def _(i):
        rows = pl.ds(pl.multiple_of(i * 32, 32), 32)
        filtered = []
        value = None
        for t in range(8):
            new = gains[t] * y_ref[t, rows, :].astype(F32)
            value = new if t == 0 else (1.0 - gains[t]) * value + new
            filtered.append(value)
        out[7, rows, :] = value.astype(BF16)
        for t in range(6, -1, -1):
            value = (1.0 - factors[t]) * filtered[t] + factors[t] * value
            out[t, rows, :] = value.astype(BF16)


def smooth(y, var, noise):
    return pl.pallas_call(
        smooth_kernel,
        out_shape=jax.ShapeDtypeStruct((8, 256, K), BF16),
        in_specs=vmem(3),
        out_specs=pl.BlockSpec(memory_space=pltpu.VMEM),
        name="smooth",
    )(y, var, noise)


def body(counts, topic_means, doc_topics_init, dirichlet_prior, chain_var, obs_noise):
    x = topic_means[0]
    y, xl, c = lax.axis_index("y"), lax.axis_index("xl"), lax.axis_index("c")
    chips = jnp.stack([lax.rem(y + dy, 4) * 2 + lax.rem(xl + dx, 2) for dy, dx in REL])
    own_at, give_at = 2 * chips + c, 2 * chips + 1 - c

    h0, h1, level = slab_softmax(x)
    beta = gather(h0, h1)

    other_init = across(doc_topics_init[0])
    mine, give = split_counts(counts[0], own_at, give_at)
    theirs = across(give)

    chip_level = jnp.logaddexp(level, across(level))
    pair = jnp.stack([level, chip_level])
    pairs = {(0, 0): pair, (0, 1): xswap(pair)}
    both = jnp.stack([pairs[0, 0], pairs[0, 1]])
    for dy in (1, 2, 3):
        got = yfrom(both, dy)
        pairs[dy, 0], pairs[dy, 1] = got[0], got[1]
    chip_levels = jnp.stack([pairs[r][1, 0] for r in REL])
    peak = jnp.max(chip_levels, axis=0, keepdims=True)
    whole = peak + jnp.log(jnp.sum(jnp.exp(chip_levels - peak), axis=0, keepdims=True))
    scale = jnp.exp(jnp.stack([pairs[r][0, 0] for r in REL]) - whole)

    prior = dirichlet_prior[None, :]
    p, part = sweep("init", (doc_topics_init[0], other_init), scale, beta, mine, theirs)
    for _ in range(ITERS_E - 2):
        p, part = sweep("parts", (part, across(part), p, prior), scale, beta, mine, theirs)

    index = {r: i for i, r in enumerate(REL)}
    orders = [[(2, 1)], [(1, 1), (3, 1), (2, 0)], [(0, 1), (1, 0), (3, 0), (0, 0)]]
    stats = {}
    parts = []
    for i, order in enumerate(orders):
        slabs = tuple(index[r] for r in order)
        if i == 0:
            p, *outs = sweep(
                "parts", (part, across(part), p, prior), scale, beta, mine, theirs, slabs, True
            )
        else:
            outs = sweep("given", (p,), scale, beta, mine, theirs, slabs, True)
        parts.append(outs[0])
        for j, r in enumerate(order):
            stats[r + (0,)], stats[r + (1,)] = outs[1 + 2 * j], outs[2 + 2 * j]
    part = parts[0] + parts[1] + parts[2]
    half0, half1 = scatter(stats)

    got = across(part)
    update = p.astype(F32) * (part + jnp.concatenate([got[DOCS:], got[:DOCS]], axis=0))
    concentration = prior + update[:DOCS]
    total = jnp.broadcast_to(jnp.sum(update, axis=0, keepdims=True), (8, K))
    total = total + xswap(total)
    total = total + yfrom(total, 1)
    total = total + yfrom(total, 2)

    rows = pseudo_rows(half0, half1, x, whole, total)
    rows = lax.all_to_all(rows, TM, 0, 0)
    smoothed = smooth(rows, chain_var[None, :], obs_noise[None, :])
    smoothed = lax.all_to_all(smoothed, TM, 0, 0)
    return smoothed.reshape(1, SLAB, K).astype(F32), concentration[None]


def solution(mesh):
    split = Mesh(mesh.devices.reshape(4, 2, 4, 2, 2), ("z", "xh", "y", "xl", "c"))
    docs = ("y", "xl", "c")
    placed = (P(TM, docs, None), P(TM, docs, None), P(TM, docs, None), P(), P(), P())
    return jax.shard_map(
        body,
        mesh=split,
        in_specs=placed,
        out_specs=(P(TM, docs, None), P(TM, docs, None)),
        check_vma=False,
    )
```

```python
import functools

import jax
import jax.numpy as jnp
from jax import lax
from jax.experimental import pallas as pl
from jax.experimental.pallas import tpu as pltpu
from jax.sharding import Mesh
from jax.sharding import PartitionSpec as P


V = 32768
K = 128
SLAB = 2048
HALF = 1024
DOCS = 64
ITERS_E = 4
TM = ("z", "xh")

prior_count = 0.5
initial_scale = 1000.0

F32 = jnp.float32
BF16 = jnp.bfloat16
GRANT = pltpu.CompilerParams(vmem_limit_bytes=16 << 20)

REL = [(dy, dx) for dy in range(4) for dx in range(2)]


def across(x):
    return lax.ppermute(x, "c", [(0, 1), (1, 0)])


def xswap(x):
    return lax.ppermute(x, "xl", [(0, 1), (1, 0)])


def yfrom(x, dy):
    return lax.ppermute(x, "y", [((i + dy) % 4, i) for i in range(4)])


def vmem(n):
    return [pl.BlockSpec(memory_space=pltpu.VMEM)] * n


def split3(x):
    hi = x.astype(BF16)
    rest = x - hi.astype(F32)
    mid = rest.astype(BF16)
    low = (rest - mid.astype(F32)).astype(BF16)
    return hi, mid, low


def slab_kernel(x_ref, b_ref, l_ref, e_ref):
    def peak(i, m):
        return jnp.maximum(m, jnp.max(x_ref[pl.ds(i * 256, 256), :].reshape(32, 8, K), axis=0))

    m8 = lax.fori_loop(0, 8, peak, jnp.full((8, K), -jnp.inf, F32))
    m = jnp.max(m8, axis=0, keepdims=True)

    def mass(i, s):
        e = jnp.exp(x_ref[pl.ds(i * 256, 256), :] - m)
        e_ref[pl.ds(i * 256, 256), :] = e
        return s + jnp.sum(e.reshape(32, 8, K), axis=0)

    s8 = lax.fori_loop(0, 8, mass, jnp.zeros((8, K), F32))
    s = jnp.sum(s8, axis=0, keepdims=True)
    inverse = 1.0 / s
    l_ref[...] = jnp.broadcast_to(m + jnp.log(s), (8, K))

    @pl.loop(0, 8)
    def _(i):
        rows = pl.ds(pl.multiple_of(i * 256, 256), 256)
        b_ref[rows, :] = (e_ref[rows, :] * inverse).astype(BF16)


def slab_softmax(x):
    return pl.pallas_call(
        slab_kernel,
        out_shape=(
            jax.ShapeDtypeStruct((SLAB, K), BF16),
            jax.ShapeDtypeStruct((8, K), F32),
        ),
        in_specs=vmem(1),
        out_specs=tuple(vmem(2)),
        scratch_shapes=[pltpu.VMEM((SLAB, K), F32)],
        compiler_params=GRANT,
        name="slab_softmax",
    )(x)


def give_kernel(at, in_ref, out_ref):
    out_ref[0] = in_ref[...].astype(F32).astype(BF16)


def give_counts(counts, at):
    spec = pltpu.PrefetchScalarGridSpec(
        num_scalar_prefetch=1,
        grid=(8,),
        in_specs=[pl.BlockSpec((DOCS, SLAB), lambda r, g: (0, g[r]))],
        out_specs=pl.BlockSpec((1, DOCS, SLAB), lambda r, g: (r, 0, 0)),
    )
    return pl.pallas_call(
        give_kernel,
        grid_spec=spec,
        out_shape=jax.ShapeDtypeStruct((8, DOCS, SLAB), BF16),
        compiler_params=GRANT,
        cost_estimate=pl.CostEstimate(flops=0, bytes_accessed=6 << 20, transcendentals=0),
        name="give_counts",
    )(at, counts)


def digamma(x):
    total = jnp.zeros_like(x)
    for i in range(8):
        total = total + 1.0 / (x + float(i))
    y = x + 8.0
    r = 1.0 / y
    r2 = r * r
    tail = r2 * (1.0 / 12.0 - r2 * (1.0 / 120.0 - r2 * (1.0 / 252.0 - r2 * (1.0 / 240.0))))
    return jnp.log(y) - 0.5 * r - tail - total


def words_of(scaled, beta, count):
    mix = lax.dot_general(scaled, beta, (((1,), (1,)), ((), ())), preferred_element_type=F32)
    return (count.astype(F32) / mix).astype(BF16)


def first_kernel(slabs, places, n_in, lead, *refs):
    n = len(slabs)
    refs = list(refs)
    if lead:
        own0, other0 = refs[:2]
        levels = refs[2:6]
        refs = refs[6:]
    else:
        given, scale_ref = refs[:2]
        refs = refs[2:]
    at_ref, counts, theirs = refs[:3]
    b_in = refs[3 : 3 + n_in]
    refs = refs[3 + n_in :]
    if lead:
        p_out, scale_out, whole_out = refs[:3]
        refs = refs[3:]
    part, bs, cs, raw, sem_b, sem_r, sem_c = refs

    copies = []
    for i, r in enumerate(slabs):
        group = []
        for h in range(2):
            source, row = places[i][h]
            group.append(
                pltpu.make_async_copy(
                    b_in[source].at[pl.ds(row, HALF)], bs.at[i, pl.ds(h * HALF, HALF)], sem_b.at[i, h]
                )
            )
        words = pl.ds(pl.multiple_of(at_ref[r] * SLAB, SLAB), SLAB)
        group.append(pltpu.make_async_copy(counts.at[:, words], raw.at[i], sem_r.at[i]))
        group.append(pltpu.make_async_copy(theirs.at[r], cs.at[i, pl.ds(DOCS, DOCS)], sem_c.at[i]))
        for copy in group:
            copy.start()
        copies.append(group)

    if lead:
        chips = [levels[dy][4 * dx + 1 : 4 * dx + 2, :] for dy, dx in REL]
        peak = functools.reduce(jnp.maximum, chips)
        mass = functools.reduce(jnp.add, [jnp.exp(chip - peak) for chip in chips])
        whole = peak + jnp.log(mass)
        whole_out[...] = jnp.broadcast_to(whole, (8, K))
        rows = [jnp.exp(levels[dy][4 * dx : 4 * dx + 1, :] - whole) for dy, dx in REL]
        for r in range(8):
            scale_out[r : r + 1, :] = rows[r]
        p = jnp.exp(digamma(jnp.concatenate([own0[...], other0[...]], axis=0))).astype(BF16)
        p_out[...] = p
    else:
        p = given[...]
        rows = [scale_ref[r : r + 1, :] for r in range(8)]
    p32 = p.astype(F32)

    total = jnp.zeros((2 * DOCS, K), F32)
    for i, r in enumerate(slabs):
        for copy in copies[i]:
            copy.wait()
        cs[i, 0:DOCS, :] = raw[i].astype(F32).astype(BF16)
        ratio = words_of((p32 * rows[r]).astype(BF16), bs[i], cs[i])
        total = total + jnp.dot(ratio, bs[i], preferred_element_type=F32) * rows[r]
    part[...] = total


def first_sweep(slabs, places, heads, at, counts, theirs, pieces):
    n, lead = len(slabs), len(heads) == 6
    outs = []
    if lead:
        outs.append(jax.ShapeDtypeStruct((2 * DOCS, K), BF16))
        outs += [jax.ShapeDtypeStruct((8, K), F32)] * 2
    outs.append(jax.ShapeDtypeStruct((2 * DOCS, K), F32))
    outs.append(jax.ShapeDtypeStruct((n, SLAB, K), BF16))
    outs.append(jax.ShapeDtypeStruct((n, 2 * DOCS, SLAB), BF16))
    anywhere = [pl.BlockSpec(memory_space=pl.ANY)]
    return pl.pallas_call(
        functools.partial(first_kernel, slabs, places, len(pieces), lead),
        out_shape=outs,
        in_specs=vmem(len(heads))
        + [pl.BlockSpec(memory_space=pltpu.SMEM)]
        + anywhere * (2 + len(pieces)),
        out_specs=vmem(len(outs)),
        scratch_shapes=[
            pltpu.VMEM((n, DOCS, SLAB), jnp.int32),
            pltpu.SemaphoreType.DMA((n, 2)),
            pltpu.SemaphoreType.DMA((n,)),
            pltpu.SemaphoreType.DMA((n,)),
        ],
        compiler_params=GRANT,
        cost_estimate=pl.CostEstimate(
            flops=4 * 2 * DOCS * K * SLAB * n,
            bytes_accessed=2 * n << 20,
            transcendentals=2 * DOCS * SLAB * n,
        ),
        name="first_sweep" + str(n),
    )(*heads, at, counts, theirs, *pieces)


def sweep_kernel(heads, slabs, stats, *refs):
    groups, lead = len(slabs), heads > 1
    refs = list(refs)
    head, scale, refs = refs[:heads], refs[heads], refs[heads + 1 :]
    bs, cs = refs[:groups], refs[groups : 2 * groups]
    refs = refs[2 * groups :]
    if lead:
        mine, got, before, prior = head
        got = got[...]
        total = mine[...] + jnp.concatenate([got[DOCS:], got[:DOCS]], axis=0)
        gamma = prior[...] + before[...].astype(F32) * total
        p = jnp.exp(digamma(gamma)).astype(BF16)
        refs.pop(0)[...] = p
    else:
        p = head[0][...]
    part = refs.pop(0)
    p32 = p.astype(F32)
    if stats:
        pt = p32.T.astype(BF16)

    steps = [(g, i, h) for g in range(groups) for i in range(len(slabs[g])) for h in range(2)]

    def mixture(g, i, h):
        scaled = (p32 * scale[slabs[g][i] : slabs[g][i] + 1, :]).astype(BF16)
        return lax.dot_general(
            scaled,
            bs[g][i, h * HALF : (h + 1) * HALF, :],
            (((1,), (1,)), ((), ())),
            preferred_element_type=F32,
        )

    total = jnp.zeros((2 * DOCS, K), F32)
    ahead = mixture(*steps[0])
    for at, (g, i, h) in enumerate(steps):
        mix = ahead
        if at + 1 < len(steps):
            ahead = mixture(*steps[at + 1])
        words = slice(h * HALF, (h + 1) * HALF)
        ratio = (cs[g][i, :, words].astype(F32) / mix).astype(BF16)
        new = jnp.dot(ratio, bs[g][i, words, :], preferred_element_type=F32)
        acc = new if h == 0 else acc + new
        if h == 1:
            total = total + acc * scale[slabs[g][i] : slabs[g][i] + 1, :]
        if stats:
            refs[2 * i + h][...] = jnp.dot(pt, ratio, preferred_element_type=F32).astype(BF16)
    part[...] = total


def sweep(heads, scale, slabs, bs, cs, stats=False):
    n = sum(len(group) for group in slabs)
    lead = len(heads) > 1
    outs = []
    if lead:
        outs.append(jax.ShapeDtypeStruct((2 * DOCS, K), BF16))
    outs.append(jax.ShapeDtypeStruct((2 * DOCS, K), F32))
    if stats:
        outs += [jax.ShapeDtypeStruct((K, HALF), BF16)] * (2 * n)
    return pl.pallas_call(
        functools.partial(sweep_kernel, len(heads), slabs, stats),
        out_shape=outs,
        in_specs=vmem(len(heads) + 1 + 2 * len(slabs)),
        out_specs=vmem(len(outs)),
        compiler_params=GRANT,
        cost_estimate=pl.CostEstimate(
            flops=(6 if stats else 4) * 2 * DOCS * K * SLAB * n,
            bytes_accessed=n << 20,
            transcendentals=2 * DOCS * SLAB * n,
        ),
        name=("stats" if stats else "sweep") + str(n),
    )(*heads, scale, *bs, *cs)


def plus(*terms):
    total = terms[0].astype(F32)
    for term in terms[1:]:
        total = total + term.astype(F32)
    return total.astype(BF16)


def scatter(s):
    down = lambda x: yfrom(x, 1)
    up = lambda x: yfrom(x, 3)
    x1 = xswap(s[2, 1, 0])
    u1 = down(s[2, 1, 1])
    x2 = xswap(s[1, 1, 0])
    d2 = up(s[1, 1, 1])
    u2 = down(plus(s[3, 1, 1], u1))
    x3 = xswap(s[3, 1, 0])
    d3 = up(s[2, 0, 1])
    u3 = down(plus(s[2, 0, 0], x1))
    u4 = down(s[3, 0, 1])
    x4 = xswap(plus(s[0, 1, 1], u2, d2))
    d4 = up(plus(s[1, 0, 0], x2))
    x5 = xswap(s[0, 1, 0])
    d5 = up(plus(s[1, 0, 1], d3))
    u5 = down(plus(s[3, 0, 0], x3, u3))
    return (s[0, 0, 0], x5, u5, d4), (s[0, 0, 1], x4, u4, d5)


def pseudo_kernel(*refs):
    halves = (refs[0:4], refs[4:8])
    x_ref, l_ref, total_ref, out = refs[8:12]
    total = total_ref[0:1, :]
    level = jnp.log((total + prior_count * V) / V)
    for h in range(2):
        for q in range(4):
            rows = slice(q * 256, (q + 1) * 256)
            acc = halves[h][0][:, rows].astype(F32)
            for ref in halves[h][1:]:
                acc = acc + ref[:, rows].astype(F32)
            x = x_ref[h * HALF + q * 256 : h * HALF + (q + 1) * 256, :]
            beta = jnp.exp(x - l_ref[0:1, :]).astype(BF16).astype(F32)
            out[4 * h + q, 0:256, :] = (jnp.log(beta * acc.T + prior_count) - level).astype(BF16)
    hi, mid, low = split3(total)
    row = lax.broadcasted_iota(jnp.int32, (16, K), 0)
    head = jnp.where(row == 0, hi.astype(F32), jnp.where(row == 1, mid.astype(F32), low.astype(F32)))
    for t in range(8):
        out[t, 256:272, :] = head.astype(BF16)


def pseudo_rows(half0, half1, x, level, total):
    return pl.pallas_call(
        pseudo_kernel,
        out_shape=jax.ShapeDtypeStruct((8, 272, K), BF16),
        in_specs=vmem(11),
        out_specs=pl.BlockSpec(memory_space=pltpu.VMEM),
        compiler_params=GRANT,
        name="pseudo_rows",
    )(*half0, *half1, x, level, total)


def smooth_kernel(y_ref, var_ref, noise_ref, out):
    var = var_ref[...]
    gains, factors = [], []
    previous = initial_scale * var
    for t in range(8):
        head = y_ref[t, 256:272, :].astype(F32)
        total = head[0:1] + head[1:2] + head[2:3]
        noise = noise_ref[...] * jnp.sum(total, axis=1, keepdims=True) / (K * total)
        predicted = previous + var
        gain = predicted / (predicted + noise)
        previous = (1.0 - gain) * predicted
        gains.append(gain)
        factors.append(previous / (previous + var))

    @pl.loop(0, 8)
    def _(i):
        rows = pl.ds(pl.multiple_of(i * 32, 32), 32)
        filtered = []
        value = None
        for t in range(8):
            new = gains[t] * y_ref[t, rows, :].astype(F32)
            value = new if t == 0 else (1.0 - gains[t]) * value + new
            filtered.append(value)
        out[7, rows, :] = value.astype(BF16)
        for t in range(6, -1, -1):
            value = (1.0 - factors[t]) * filtered[t] + factors[t] * value
            out[t, rows, :] = value.astype(BF16)


def smooth(y, var, noise):
    return pl.pallas_call(
        smooth_kernel,
        out_shape=jax.ShapeDtypeStruct((8, 256, K), BF16),
        in_specs=vmem(3),
        out_specs=pl.BlockSpec(memory_space=pltpu.VMEM),
        compiler_params=GRANT,
        name="smooth",
    )(y, var, noise)


def body(counts, topic_means, doc_topics_init, dirichlet_prior, chain_var, obs_noise):
    x = topic_means[0]
    y, xl, c = lax.axis_index("y"), lax.axis_index("xl"), lax.axis_index("c")
    chips = jnp.stack([lax.rem(y + dy, 4) * 2 + lax.rem(xl + dx, 2) for dy, dx in REL])
    counts = counts[0]
    init = doc_topics_init[0]

    b, level = slab_softmax(x)
    bx, bu, bd = xswap(b), yfrom(b, 3), yfrom(b, 1)
    other_init = across(init)
    theirs = across(give_counts(counts, 2 * chips + 1 - c))

    row = lax.broadcasted_iota(jnp.int32, (8, K), 0)
    pair = jnp.where(row % 2 == 0, level, jnp.logaddexp(level, across(level)))
    levels = [jnp.where(row < 4, pair, xswap(pair))]
    levels += [yfrom(levels[0], dy) for dy in (1, 2, 3)]

    join = lambda p, i, q, j: jnp.concatenate([p[i * HALF : (i + 1) * HALF], q[j * HALF : (j + 1) * HALF]])
    cx = xswap(join(bu, 0, bd, 0))
    cu = yfrom(join(bu, 0, bx, 1), 3)
    cd = yfrom(join(bd, 1, bx, 1), 1)
    ex = xswap(cu[:HALF])
    eu = yfrom(cu[HALF:], 3)

    index = {r: i for i, r in enumerate(REL)}
    orders = [[(0, 0), (0, 1), (3, 0), (1, 0)], [(2, 0), (3, 1), (1, 1)], [(2, 1)]]
    pieces = [(b, bx, bu, bd), (cx, cu, cd), (ex, eu)]
    places = [
        [((i, 0), (i, HALF)) for i in range(4)],
        [((1, 0), (2, 0)), ((0, 0), (1, HALF)), ((0, HALF), (2, HALF))],
        [((0, 0), (1, 0))],
    ]
    slabs = tuple(tuple(index[r] for r in order) for order in orders)
    heads = (init, other_init, *levels)
    bs, cs, parts = [], [], []
    for g in range(3):
        outs = first_sweep(
            slabs[g], places[g], heads, 2 * chips + c, counts, theirs, pieces[g]
        )
        if g == 0:
            p, scale, whole, *outs = outs
            heads = (p, scale)
        parts.append(outs[0])
        bs.append(outs[1])
        cs.append(outs[2])
    part = parts[0] + parts[1] + parts[2]

    prior = dirichlet_prior[None, :]
    for _ in range(ITERS_E - 2):
        p, part = sweep((part, across(part), p, prior), scale, slabs, bs, cs)

    stats = {}
    parts = []
    heads = (part, across(part), p, prior)
    for g in (2, 1, 0):
        outs = sweep(heads, scale, slabs[g : g + 1], bs[g : g + 1], cs[g : g + 1], True)
        if g == 2:
            p, *outs = outs
            heads = (p,)
        parts.append(outs[0])
        for j, r in enumerate(orders[g]):
            stats[r + (0,)], stats[r + (1,)] = outs[1 + 2 * j], outs[2 + 2 * j]
    part = parts[0] + parts[1] + parts[2]
    half0, half1 = scatter(stats)

    got = across(part)
    update = p.astype(F32) * (part + jnp.concatenate([got[DOCS:], got[:DOCS]], axis=0))
    concentration = prior + update[:DOCS]
    total = jnp.broadcast_to(jnp.sum(update, axis=0, keepdims=True), (8, K))
    total = total + xswap(total)
    total = total + yfrom(total, 1)
    total = total + yfrom(total, 2)

    rows = pseudo_rows(half0, half1, x, whole, total)
    rows = lax.all_to_all(rows, TM, 0, 0)
    smoothed = smooth(rows, chain_var[None, :], obs_noise[None, :])
    smoothed = lax.all_to_all(smoothed, TM, 0, 0)
    return smoothed.reshape(1, SLAB, K).astype(F32), concentration[None]


def solution(mesh):
    split = Mesh(mesh.devices.reshape(4, 2, 4, 2, 2), ("z", "xh", "y", "xl", "c"))
    docs = ("y", "xl", "c")
    placed = (P(TM, docs, None), P(TM, docs, None), P(TM, docs, None), P(), P(), P())
    return jax.shard_map(
        body,
        mesh=split,
        in_specs=placed,
        out_specs=(P(TM, docs, None), P(TM, docs, None)),
        check_vma=False,
    )
```

```python
import functools

import jax
import jax.numpy as jnp
from jax import lax
from jax.experimental import pallas as pl
from jax.experimental.pallas import tpu as pltpu
from jax.sharding import Mesh
from jax.sharding import PartitionSpec as P


V = 32768
K = 128
SLAB = 2048
HALF = 1024
HELD = 3
DOCS = 64
ITERS_E = 4
TM = ("z", "xh")

prior_count = 0.5
initial_scale = 1000.0

F32 = jnp.float32
BF16 = jnp.bfloat16
GRANT = pltpu.CompilerParams(vmem_limit_bytes=16 << 20)

REL = [(dy, dx) for dy in range(4) for dx in range(2)]


def across(x):
    return lax.ppermute(x, "c", [(0, 1), (1, 0)])


def xswap(x):
    return lax.ppermute(x, "xl", [(0, 1), (1, 0)])


def yfrom(x, dy):
    return lax.ppermute(x, "y", [((i + dy) % 4, i) for i in range(4)])


def vmem(n):
    return [pl.BlockSpec(memory_space=pltpu.VMEM)] * n


def split3(x):
    hi = x.astype(BF16)
    rest = x - hi.astype(F32)
    mid = rest.astype(BF16)
    low = (rest - mid.astype(F32)).astype(BF16)
    return hi, mid, low


def slab_kernel(x_ref, b_ref, b0_ref, b1_ref, l_ref, e_ref):
    def peak(i, m):
        return jnp.maximum(m, jnp.max(x_ref[pl.ds(i * 256, 256), :].reshape(32, 8, K), axis=0))

    m8 = lax.fori_loop(0, 8, peak, jnp.full((8, K), -jnp.inf, F32))
    m = jnp.max(m8, axis=0, keepdims=True)

    def mass(i, s):
        e = jnp.exp(x_ref[pl.ds(i * 256, 256), :] - m)
        e_ref[pl.ds(i * 256, 256), :] = e
        return s + jnp.sum(e.reshape(32, 8, K), axis=0)

    s8 = lax.fori_loop(0, 8, mass, jnp.zeros((8, K), F32))
    s = jnp.sum(s8, axis=0, keepdims=True)
    inverse = 1.0 / s
    l_ref[...] = jnp.broadcast_to(m + jnp.log(s), (8, K))

    for h, half in enumerate((b0_ref, b1_ref)):

        @pl.loop(0, 4)
        def _(i, h=h, half=half):
            rows = pl.ds(pl.multiple_of(h * HALF + i * 256, 256), 256)
            beta = (e_ref[rows, :] * inverse).astype(BF16)
            b_ref[rows, :] = beta
            half[pl.ds(pl.multiple_of(i * 256, 256), 256), :] = beta


def slab_softmax(x):
    return pl.pallas_call(
        slab_kernel,
        out_shape=(
            jax.ShapeDtypeStruct((SLAB, K), BF16),
            jax.ShapeDtypeStruct((HALF, K), BF16),
            jax.ShapeDtypeStruct((HALF, K), BF16),
            jax.ShapeDtypeStruct((8, K), F32),
        ),
        in_specs=vmem(1),
        out_specs=tuple(vmem(4)),
        scratch_shapes=[pltpu.VMEM((SLAB, K), F32)],
        compiler_params=GRANT,
        name="slab_softmax",
    )(x)


def digamma(x):
    total = jnp.zeros_like(x)
    for i in range(8):
        total = total + 1.0 / (x + float(i))
    y = x + 8.0
    r = 1.0 / y
    r2 = r * r
    tail = r2 * (1.0 / 12.0 - r2 * (1.0 / 120.0 - r2 * (1.0 / 252.0 - r2 * (1.0 / 240.0))))
    return jnp.log(y) - 0.5 * r - tail - total


def words_of(scaled, beta, count):
    mix = lax.dot_general(scaled, beta, (((1,), (1,)), ((), ())), preferred_element_type=F32)
    return (count.astype(F32) / mix).astype(BF16)


def first_kernel(slabs, fetch, places, n_in, lead, *refs):
    n = len(slabs)
    refs = list(refs)
    if lead:
        inits, levels = refs[:2], refs[2:6]
        refs = refs[6:]
    else:
        given, scale_ref = refs[:2]
        refs = refs[2:]
    if fetch:
        at_ref, counts, theirs = refs[:3]
        refs = refs[3:]
    else:
        cs, refs = refs[0].at[pl.ds(HELD, 1)], refs[1:]
    b_in = refs[:n_in]
    refs = refs[n_in:]
    if lead:
        p_out, scale_out, whole_out = refs[:3]
        refs = refs[3:]
    part, bs = refs[:2]
    if fetch:
        cs, raw, sem_r = refs[2:5]
        refs = refs[3:]
    sem_b = refs[2]

    if lead:
        gamma, sem_g = refs[3:]
        starts = [
            pltpu.make_async_copy(ref, gamma.at[pl.ds(side * DOCS, DOCS)], sem_g.at[side])
            for side, ref in enumerate(inits)
        ]
        for copy in starts:
            copy.start()

    copies = []
    for i, r in enumerate(slabs):
        group = []
        for h in range(2):
            source, row = places[i][h]
            group.append(
                pltpu.make_async_copy(
                    b_in[source].at[pl.ds(row, HALF)], bs.at[i, pl.ds(h * HALF, HALF)], sem_b.at[i, h]
                )
            )
        copies.append(group)
    for i, r in enumerate(fetch):
        if i >= n:
            copies.append([])
        words = pl.ds(pl.multiple_of(at_ref[r] * SLAB, SLAB), SLAB)
        for side, ref in enumerate((counts, theirs)):
            copies[i].append(
                pltpu.make_async_copy(
                    ref.at[:, words], raw.at[i, pl.ds(side * DOCS, DOCS)], sem_r.at[i, side]
                )
            )
    for group in copies:
        for copy in group:
            copy.start()

    if lead:
        chips = [levels[dy][4 * dx + 1 : 4 * dx + 2, :] for dy, dx in REL]
        peak = functools.reduce(jnp.maximum, chips)
        mass = functools.reduce(jnp.add, [jnp.exp(chip - peak) for chip in chips])
        whole = peak + jnp.log(mass)
        whole_out[...] = jnp.broadcast_to(whole, (8, K))
        rows = [jnp.exp(levels[dy][4 * dx : 4 * dx + 1, :] - whole) for dy, dx in REL]
        for r in range(8):
            scale_out[r : r + 1, :] = rows[r]
        for copy in starts:
            copy.wait()
        p = jnp.exp(digamma(gamma[...])).astype(BF16)
        p_out[...] = p
    else:
        p = given[...]
        rows = [scale_ref[r : r + 1, :] for r in range(8)]
    p32 = p.astype(F32)

    total = jnp.zeros((2 * DOCS, K), F32)
    for i, r in enumerate(slabs):
        for copy in copies[i]:
            copy.wait()
        if fetch:
            cs[i] = raw[i].astype(F32).astype(BF16)
        ratio = words_of((p32 * rows[r]).astype(BF16), bs[i], cs[i])
        total = total + jnp.dot(ratio, bs[i], preferred_element_type=F32) * rows[r]
    part[...] = total
    for i in range(n, len(fetch)):
        for copy in copies[i]:
            copy.wait()
        cs[i] = raw[i].astype(F32).astype(BF16)


def first_sweep(slabs, fetch, places, heads, counts, pieces):
    n, lead = len(slabs), len(heads) == 6
    outs = []
    if lead:
        outs.append(jax.ShapeDtypeStruct((2 * DOCS, K), BF16))
        outs += [jax.ShapeDtypeStruct((8, K), F32)] * 2
    outs.append(jax.ShapeDtypeStruct((2 * DOCS, K), F32))
    outs.append(jax.ShapeDtypeStruct((n, SLAB, K), BF16))
    if fetch:
        outs.append(jax.ShapeDtypeStruct((len(fetch), 2 * DOCS, SLAB), BF16))
    anywhere = [pl.BlockSpec(memory_space=pl.ANY)]
    return pl.pallas_call(
        functools.partial(first_kernel, slabs, fetch, places, len(pieces), lead),
        out_shape=outs,
        in_specs=(anywhere * 2 + vmem(4) if lead else vmem(2))
        + ([pl.BlockSpec(memory_space=pltpu.SMEM)] + anywhere * 2 if fetch else vmem(1))
        + anywhere * len(pieces),
        out_specs=vmem(len(outs)),
        scratch_shapes=[
            pltpu.VMEM((len(fetch), 2 * DOCS, SLAB), jnp.int32),
            pltpu.SemaphoreType.DMA((len(fetch), 2)),
        ][: 2 if fetch else 0]
        + [pltpu.SemaphoreType.DMA((n, 2))]
        + ([pltpu.VMEM((2 * DOCS, K), F32), pltpu.SemaphoreType.DMA((2,))] if lead else []),
        compiler_params=GRANT,
        cost_estimate=pl.CostEstimate(
            flops=4 * 2 * DOCS * K * SLAB * n,
            bytes_accessed=2 * n << 20,
            transcendentals=2 * DOCS * SLAB * n,
        ),
    )(*heads, *counts, *pieces)


def sweep_kernel(heads, slabs, stats, *refs):
    groups, lead = len(slabs), heads > 1
    refs = list(refs)
    head, scale, refs = refs[:heads], refs[heads], refs[heads + 1 :]
    bs, cs = refs[:groups], refs[groups : 2 * groups]
    refs = refs[2 * groups :]
    if lead:
        mine, got, before, prior = head
        got = got[...]
        total = mine[...] + jnp.concatenate([got[DOCS:], got[:DOCS]], axis=0)
        gamma = prior[...] + before[...].astype(F32) * total
        p = jnp.exp(digamma(gamma)).astype(BF16)
        refs.pop(0)[...] = p
    else:
        p = head[0][...]
    part = refs.pop(0)
    p32 = p.astype(F32)
    if stats:
        pt = p32.T.astype(BF16)

    steps = [(g, i, h) for g in range(groups) for i in range(len(slabs[g])) for h in range(2)]

    def mixture(g, i, h):
        scaled = (p32 * scale[slabs[g][i] : slabs[g][i] + 1, :]).astype(BF16)
        return lax.dot_general(
            scaled,
            bs[g][i, h * HALF : (h + 1) * HALF, :],
            (((1,), (1,)), ((), ())),
            preferred_element_type=F32,
        )

    total = jnp.zeros((2 * DOCS, K), F32)
    ahead = mixture(*steps[0])
    for at, (g, i, h) in enumerate(steps):
        mix = ahead
        if at + 1 < len(steps):
            ahead = mixture(*steps[at + 1])
        words = slice(h * HALF, (h + 1) * HALF)
        count = cs[g][i + (HELD if len(slabs[g]) == 1 else 0), :, words]
        ratio = (count.astype(F32) / mix).astype(BF16)
        new = jnp.dot(ratio, bs[g][i, words, :], preferred_element_type=F32)
        acc = new if h == 0 else acc + new
        if h == 1:
            total = total + acc * scale[slabs[g][i] : slabs[g][i] + 1, :]
        if stats:
            refs[2 * i + h][...] = jnp.dot(pt, ratio, preferred_element_type=F32).astype(BF16)
    part[...] = total


def sweep(heads, scale, slabs, bs, cs, stats=False):
    n = sum(len(group) for group in slabs)
    lead = len(heads) > 1
    outs = []
    if lead:
        outs.append(jax.ShapeDtypeStruct((2 * DOCS, K), BF16))
    outs.append(jax.ShapeDtypeStruct((2 * DOCS, K), F32))
    if stats:
        outs += [jax.ShapeDtypeStruct((K, HALF), BF16)] * (2 * n)
    return pl.pallas_call(
        functools.partial(sweep_kernel, len(heads), slabs, stats),
        out_shape=outs,
        in_specs=vmem(len(heads) + 1 + 2 * len(slabs)),
        out_specs=vmem(len(outs)),
        compiler_params=GRANT,
        cost_estimate=pl.CostEstimate(
            flops=(6 if stats else 4) * 2 * DOCS * K * SLAB * n,
            bytes_accessed=n << 20,
            transcendentals=2 * DOCS * SLAB * n,
        ),
    )(*heads, scale, *bs, *cs)


def plus(*terms):
    total = terms[0].astype(F32)
    for term in terms[1:]:
        total = total + term.astype(F32)
    return total.astype(BF16)


def scatter(s):
    down = lambda x: yfrom(x, 1)
    up = lambda x: yfrom(x, 3)
    x1 = xswap(s[2, 1, 0])
    u1 = down(s[2, 1, 1])
    x2 = xswap(s[1, 1, 0])
    d2 = up(s[1, 1, 1])
    u2 = down(plus(s[3, 1, 1], u1))
    x3 = xswap(s[3, 1, 0])
    d3 = up(s[2, 0, 1])
    u3 = down(plus(s[2, 0, 0], x1))
    u4 = down(s[3, 0, 1])
    x4 = xswap(plus(s[0, 1, 1], u2, d2))
    d4 = up(plus(s[1, 0, 0], x2))
    x5 = xswap(s[0, 1, 0])
    d5 = up(plus(s[1, 0, 1], d3))
    u5 = down(plus(s[3, 0, 0], x3, u3))
    return (s[0, 0, 0], x5, u5, d4), (s[0, 0, 1], x4, u4, d5)


def pseudo_kernel(*refs):
    halves = (refs[0:4], refs[4:8])
    x_ref, l_ref, total_ref, out = refs[8:12]
    total = total_ref[0:1, :]
    level = jnp.log((total + prior_count * V) / V)
    for h in range(2):
        for q in range(4):
            rows = slice(q * 256, (q + 1) * 256)
            acc = halves[h][0][:, rows].astype(F32)
            for ref in halves[h][1:]:
                acc = acc + ref[:, rows].astype(F32)
            x = x_ref[h * HALF + q * 256 : h * HALF + (q + 1) * 256, :]
            beta = jnp.exp(x - l_ref[0:1, :]).astype(BF16).astype(F32)
            out[4 * h + q, 0:256, :] = (jnp.log(beta * acc.T + prior_count) - level).astype(BF16)
    hi, mid, low = split3(total)
    row = lax.broadcasted_iota(jnp.int32, (16, K), 0)
    head = jnp.where(row == 0, hi.astype(F32), jnp.where(row == 1, mid.astype(F32), low.astype(F32)))
    for t in range(8):
        out[t, 256:272, :] = head.astype(BF16)


def pseudo_rows(half0, half1, x, level, total):
    return pl.pallas_call(
        pseudo_kernel,
        out_shape=jax.ShapeDtypeStruct((8, 272, K), BF16),
        in_specs=vmem(11),
        out_specs=pl.BlockSpec(memory_space=pltpu.VMEM),
        compiler_params=GRANT,
        name="pseudo_rows",
    )(*half0, *half1, x, level, total)


def smooth_kernel(y_ref, var_ref, noise_ref, out):
    var = var_ref[...]
    gains, factors = [], []
    previous = initial_scale * var
    for t in range(8):
        head = y_ref[t, 256:272, :].astype(F32)
        total = head[0:1] + head[1:2] + head[2:3]
        noise = noise_ref[...] * jnp.sum(total, axis=1, keepdims=True) / (K * total)
        predicted = previous + var
        gain = predicted / (predicted + noise)
        previous = (1.0 - gain) * predicted
        gains.append(gain)
        factors.append(previous / (previous + var))

    @pl.loop(0, 8)
    def _(i):
        rows = pl.ds(pl.multiple_of(i * 32, 32), 32)
        filtered = []
        value = None
        for t in range(8):
            new = gains[t] * y_ref[t, rows, :].astype(F32)
            value = new if t == 0 else (1.0 - gains[t]) * value + new
            filtered.append(value)
        out[7, rows, :] = value.astype(BF16)
        for t in range(6, -1, -1):
            value = (1.0 - factors[t]) * filtered[t] + factors[t] * value
            out[t, rows, :] = value.astype(BF16)


def smooth(y, var, noise):
    return pl.pallas_call(
        smooth_kernel,
        out_shape=jax.ShapeDtypeStruct((8, 256, K), BF16),
        in_specs=vmem(3),
        out_specs=pl.BlockSpec(memory_space=pltpu.VMEM),
        compiler_params=GRANT,
        name="smooth",
    )(y, var, noise)


def body(counts, topic_means, doc_topics_init, dirichlet_prior, chain_var, obs_noise):
    x = topic_means[0]
    y, xl, c = lax.axis_index("y"), lax.axis_index("xl"), lax.axis_index("c")
    chips = jnp.stack([lax.rem(y + dy, 4) * 2 + lax.rem(xl + dx, 2) for dy, dx in REL])
    counts = counts[0]
    init = doc_topics_init[0]

    b, b0, b1, level = slab_softmax(x)
    bx = xswap(b)
    u0, u1 = yfrom(b0, 3), yfrom(b1, 3)
    d0, d1 = yfrom(b0, 1), yfrom(b1, 1)
    other_init = across(init)
    theirs = across(counts)

    row = lax.broadcasted_iota(jnp.int32, (8, K), 0)
    pair = jnp.where(row % 2 == 0, level, jnp.logaddexp(level, across(level)))
    far = xswap(pair)
    levels = [jnp.where(row < 4, pair, far)]
    levels += [yfrom(levels[0], dy) for dy in (1, 2, 3)]

    x31, u20, d20 = xswap(u0), yfrom(u0, 3), yfrom(d1, 1)
    u31, d11 = yfrom(bx[HALF:], 3), yfrom(bx[HALF:], 1)
    x11 = xswap(d0)
    x21, u21 = xswap(u20), yfrom(u31, 3)

    index = {r: i for i, r in enumerate(REL)}
    orders = [[(0, 0), (0, 1), (3, 0), (1, 0)], [(2, 0), (3, 1), (1, 1)], [(2, 1)]]
    pieces = [(b, bx, u0, u1, d0, d1), (u20, d20, x31, u31, x11, d11), (x21, u21)]
    places = [
        [((0, 0), (0, HALF)), ((1, 0), (1, HALF)), ((2, 0), (3, 0)), ((4, 0), (5, 0))],
        [((0, 0), (1, 0)), ((2, 0), (3, 0)), ((4, 0), (5, 0))],
        [((0, 0), (1, 0))],
    ]
    slabs = tuple(tuple(index[r] for r in order) for order in orders)
    fetches = (slabs[0], slabs[1] + slabs[2], ())
    stay = lambda a: pltpu.with_memory_space_constraint(a, pltpu.HBM)
    heads = (stay(init), stay(other_init), *levels)
    given = (2 * chips + c, stay(counts), stay(theirs))
    bs, cs, parts = [], [], []
    for g in range(3):
        outs = first_sweep(
            slabs[g], fetches[g], places[g], heads, cs[1:] if g == 2 else given, pieces[g]
        )
        if g == 0:
            p, scale, whole, *outs = outs
            heads = (p, scale)
        parts.append(outs[0])
        bs.append(outs[1])
        cs.append(outs[2] if g < 2 else cs[1])
    part = parts[0] + parts[1] + parts[2]

    prior = dirichlet_prior[None, :]
    for _ in range(ITERS_E - 2):
        p, part = sweep((part, across(part), p, prior), scale, slabs, bs, cs)

    stats = {}
    parts = []
    heads = (part, across(part), p, prior)
    for g in (2, 1, 0):
        outs = sweep(heads, scale, slabs[g : g + 1], bs[g : g + 1], cs[g : g + 1], True)
        if g == 2:
            p, *outs = outs
            heads = (p,)
        parts.append(outs[0])
        for j, r in enumerate(orders[g]):
            stats[r + (0,)], stats[r + (1,)] = outs[1 + 2 * j], outs[2 + 2 * j]
    part = parts[0] + parts[1] + parts[2]
    half0, half1 = scatter(stats)

    got = across(part)
    update = p.astype(F32) * (part + jnp.concatenate([got[DOCS:], got[:DOCS]], axis=0))
    concentration = prior + update[:DOCS]
    total = jnp.broadcast_to(jnp.sum(update, axis=0, keepdims=True), (8, K))
    total = total + xswap(total)
    total = total + yfrom(total, 3)
    total = total + yfrom(total, 2)

    rows = pseudo_rows(half0, half1, x, whole, total)
    rows = lax.all_to_all(rows, TM, 0, 0)
    smoothed = smooth(rows, chain_var[None, :], obs_noise[None, :])
    smoothed = lax.all_to_all(smoothed, TM, 0, 0)
    return smoothed.reshape(1, SLAB, K).astype(F32), concentration[None]


def solution(mesh):
    split = Mesh(mesh.devices.reshape(4, 2, 4, 2, 2), ("z", "xh", "y", "xl", "c"))
    docs = ("y", "xl", "c")
    placed = (P(TM, docs, None), P(TM, docs, None), P(TM, docs, None), P(), P(), P())

    return jax.shard_map(
        body,
        mesh=split,
        in_specs=placed,
        out_specs=(P(TM, docs, None), P(TM, docs, None)),
        check_vma=False,
    )
```

```python
import functools

import jax
import jax.numpy as jnp
from jax import lax
from jax.experimental import pallas as pl
from jax.experimental.pallas import tpu as pltpu
from jax.sharding import Mesh
from jax.sharding import PartitionSpec as P


V = 32768
K = 128
SLAB = 2048
HALF = 1024
HELD = 3
DOCS = 64
ITERS_E = 4
TM = ("z", "xh")

prior_count = 0.5
initial_scale = 1000.0

F32 = jnp.float32
BF16 = jnp.bfloat16
GRANT = pltpu.CompilerParams(vmem_limit_bytes=16 << 20)

REL = [(dy, dx) for dy in range(4) for dx in range(2)]


def across(x):
    return lax.ppermute(x, "c", [(0, 1), (1, 0)])


def xswap(x):
    return lax.ppermute(x, "xl", [(0, 1), (1, 0)])


def yfrom(x, dy):
    return lax.ppermute(x, "y", [((i + dy) % 4, i) for i in range(4)])


def vmem(n):
    return [pl.BlockSpec(memory_space=pltpu.VMEM)] * n


def split3(x):
    hi = x.astype(BF16)
    rest = x - hi.astype(F32)
    mid = rest.astype(BF16)
    low = (rest - mid.astype(F32)).astype(BF16)
    return hi, mid, low


def slab_kernel(x_ref, b_ref, b0_ref, b1_ref, l_ref, e_ref):
    def peak(i, m):
        return jnp.maximum(m, jnp.max(x_ref[pl.ds(i * 256, 256), :].reshape(32, 8, K), axis=0))

    m8 = lax.fori_loop(0, 8, peak, jnp.full((8, K), -jnp.inf, F32))
    m = jnp.max(m8, axis=0, keepdims=True)

    def mass(i, s):
        e = jnp.exp(x_ref[pl.ds(i * 256, 256), :] - m)
        e_ref[pl.ds(i * 256, 256), :] = e
        return s + jnp.sum(e.reshape(32, 8, K), axis=0)

    s8 = lax.fori_loop(0, 8, mass, jnp.zeros((8, K), F32))
    s = jnp.sum(s8, axis=0, keepdims=True)
    inverse = 1.0 / s
    l_ref[...] = jnp.broadcast_to(m + jnp.log(s), (8, K))

    for h, half in enumerate((b0_ref, b1_ref)):

        @pl.loop(0, 4)
        def _(i, h=h, half=half):
            rows = pl.ds(pl.multiple_of(h * HALF + i * 256, 256), 256)
            beta = (e_ref[rows, :] * inverse).astype(BF16)
            b_ref[rows, :] = beta
            half[pl.ds(pl.multiple_of(i * 256, 256), 256), :] = beta


def slab_softmax(x):
    return pl.pallas_call(
        slab_kernel,
        out_shape=(
            jax.ShapeDtypeStruct((SLAB, K), BF16),
            jax.ShapeDtypeStruct((HALF, K), BF16),
            jax.ShapeDtypeStruct((HALF, K), BF16),
            jax.ShapeDtypeStruct((8, K), F32),
        ),
        in_specs=vmem(1),
        out_specs=tuple(vmem(4)),
        scratch_shapes=[pltpu.VMEM((SLAB, K), F32)],
        compiler_params=GRANT,
        name="slab_softmax",
    )(x)


def digamma(x):
    total = jnp.zeros_like(x)
    for i in range(8):
        total = total + 1.0 / (x + float(i))
    y = x + 8.0
    r = 1.0 / y
    r2 = r * r
    tail = r2 * (1.0 / 12.0 - r2 * (1.0 / 120.0 - r2 * (1.0 / 252.0 - r2 * (1.0 / 240.0))))
    return jnp.log(y) - 0.5 * r - tail - total


def words_of(scaled, beta, count):
    mix = lax.dot_general(scaled, beta, (((1,), (1,)), ((), ())), preferred_element_type=F32)
    return (count.astype(F32) / mix).astype(BF16)


def first_kernel(slabs, fetch, places, n_in, lead, *refs):
    n = len(slabs)
    refs = list(refs)
    if lead:
        inits, levels = refs[:2], refs[2:6]
        refs = refs[6:]
    else:
        given, scale_ref = refs[:2]
        refs = refs[2:]
    if fetch:
        at_ref, counts, theirs = refs[:3]
        refs = refs[3:]
    else:
        cs, refs = refs[0].at[pl.ds(HELD, 1)], refs[1:]
    b_in = refs[:n_in]
    refs = refs[n_in:]
    if lead:
        p_out, scale_out, whole_out = refs[:3]
        refs = refs[3:]
    part, bs = refs[:2]
    if fetch:
        cs, raw, sem_r = refs[2:5]
        refs = refs[3:]
    sem_b = refs[2]

    if lead:
        gamma, sem_g = refs[3:]
        starts = [
            pltpu.make_async_copy(ref, gamma.at[pl.ds(side * DOCS, DOCS)], sem_g.at[side])
            for side, ref in enumerate(inits)
        ]
        for copy in starts:
            copy.start()

    copies = []
    for i, r in enumerate(slabs):
        group = []
        for h in range(2):
            source, row = places[i][h]
            group.append(
                pltpu.make_async_copy(
                    b_in[source].at[pl.ds(row, HALF)], bs.at[i, pl.ds(h * HALF, HALF)], sem_b.at[i, h]
                )
            )
        copies.append(group)
    for i, r in enumerate(fetch):
        if i >= n:
            copies.append([])
        words = pl.ds(pl.multiple_of(at_ref[r] * SLAB, SLAB), SLAB)
        for side, ref in enumerate((counts, theirs)):
            copies[i].append(
                pltpu.make_async_copy(
                    ref.at[:, words], raw.at[i, pl.ds(side * DOCS, DOCS)], sem_r.at[i, side]
                )
            )
    for group in copies:
        for copy in group:
            copy.start()

    if lead:
        chips = [levels[dy][4 * dx + 1 : 4 * dx + 2, :] for dy, dx in REL]
        peak = functools.reduce(jnp.maximum, chips)
        mass = functools.reduce(jnp.add, [jnp.exp(chip - peak) for chip in chips])
        whole = peak + jnp.log(mass)
        whole_out[...] = jnp.broadcast_to(whole, (8, K))
        rows = [jnp.exp(levels[dy][4 * dx : 4 * dx + 1, :] - whole) for dy, dx in REL]
        for r in range(8):
            scale_out[r : r + 1, :] = rows[r]
        for copy in starts:
            copy.wait()
        p = jnp.exp(digamma(gamma[...])).astype(BF16)
        p_out[...] = p
    else:
        p = given[...]
        rows = [scale_ref[r : r + 1, :] for r in range(8)]
    p32 = p.astype(F32)

    total = jnp.zeros((2 * DOCS, K), F32)
    for i, r in enumerate(slabs):
        for copy in copies[i]:
            copy.wait()
        if fetch:
            cs[i] = raw[i].astype(F32).astype(BF16)
        ratio = words_of((p32 * rows[r]).astype(BF16), bs[i], cs[i])
        total = total + jnp.dot(ratio, bs[i], preferred_element_type=F32) * rows[r]
    part[...] = total
    for i in range(n, len(fetch)):
        for copy in copies[i]:
            copy.wait()
        cs[i] = raw[i].astype(F32).astype(BF16)


def first_sweep(slabs, fetch, places, heads, counts, pieces):
    n, lead = len(slabs), len(heads) == 6
    outs = []
    if lead:
        outs.append(jax.ShapeDtypeStruct((2 * DOCS, K), BF16))
        outs += [jax.ShapeDtypeStruct((8, K), F32)] * 2
    outs.append(jax.ShapeDtypeStruct((2 * DOCS, K), F32))
    outs.append(jax.ShapeDtypeStruct((n, SLAB, K), BF16))
    if fetch:
        outs.append(jax.ShapeDtypeStruct((len(fetch), 2 * DOCS, SLAB), BF16))
    anywhere = [pl.BlockSpec(memory_space=pl.ANY)]
    return pl.pallas_call(
        functools.partial(first_kernel, slabs, fetch, places, len(pieces), lead),
        out_shape=outs,
        in_specs=(anywhere * 2 + vmem(4) if lead else vmem(2))
        + ([pl.BlockSpec(memory_space=pltpu.SMEM)] + anywhere * 2 if fetch else vmem(1))
        + anywhere * len(pieces),
        out_specs=vmem(len(outs)),
        scratch_shapes=[
            pltpu.VMEM((len(fetch), 2 * DOCS, SLAB), jnp.int32),
            pltpu.SemaphoreType.DMA((len(fetch), 2)),
        ][: 2 if fetch else 0]
        + [pltpu.SemaphoreType.DMA((n, 2))]
        + ([pltpu.VMEM((2 * DOCS, K), F32), pltpu.SemaphoreType.DMA((2,))] if lead else []),
        compiler_params=GRANT,
        cost_estimate=pl.CostEstimate(
            flops=4 * 2 * DOCS * K * SLAB * n,
            bytes_accessed=2 * n << 20,
            transcendentals=2 * DOCS * SLAB * n,
        ),
    )(*heads, *counts, *pieces)


def sweep_kernel(heads, slabs, stats, *refs):
    groups, lead = len(slabs), heads > 1
    refs = list(refs)
    head, scale, refs = refs[:heads], refs[heads], refs[heads + 1 :]
    bs, cs = refs[:groups], refs[groups : 2 * groups]
    refs = refs[2 * groups :]
    if lead:
        mine, got, before, prior = head
        got = got[...]
        total = mine[...] + jnp.concatenate([got[DOCS:], got[:DOCS]], axis=0)
        gamma = prior[...] + before[...].astype(F32) * total
        p = jnp.exp(digamma(gamma)).astype(BF16)
        refs.pop(0)[...] = p
    else:
        p = head[0][...]
    part = refs.pop(0)
    p32 = p.astype(F32)
    if stats:
        pt = p32.T.astype(BF16)

    steps = [(g, i, h) for g in range(groups) for i in range(len(slabs[g])) for h in range(2)]

    def mixture(g, i, h):
        r, at_b, _ = slabs[g][i]
        scaled = (p32 * scale[r : r + 1, :]).astype(BF16)
        return lax.dot_general(
            scaled,
            bs[g][at_b, h * HALF : (h + 1) * HALF, :],
            (((1,), (1,)), ((), ())),
            preferred_element_type=F32,
        )

    total = jnp.zeros((2 * DOCS, K), F32)
    ahead = mixture(*steps[0])
    for at, (g, i, h) in enumerate(steps):
        mix = ahead
        if at + 1 < len(steps):
            ahead = mixture(*steps[at + 1])
        r, at_b, at_c = slabs[g][i]
        words = slice(h * HALF, (h + 1) * HALF)
        ratio = (cs[g][at_c, :, words].astype(F32) / mix).astype(BF16)
        new = jnp.dot(ratio, bs[g][at_b, words, :], preferred_element_type=F32)
        acc = new if h == 0 else acc + new
        if h == 1:
            total = total + acc * scale[r : r + 1, :]
        if stats:
            refs[at][...] = jnp.dot(pt, ratio, preferred_element_type=F32).astype(BF16)
    part[...] = total


def sweep(heads, scale, slabs, bs, cs, stats=""):
    n = sum(len(group) for group in slabs)
    lead = len(heads) > 1
    outs = []
    if lead:
        outs.append(jax.ShapeDtypeStruct((2 * DOCS, K), BF16))
    outs.append(jax.ShapeDtypeStruct((2 * DOCS, K), F32))
    if stats:
        outs += [jax.ShapeDtypeStruct((K, HALF), BF16)] * (2 * n)
    return pl.pallas_call(
        functools.partial(sweep_kernel, len(heads), slabs, bool(stats)),
        out_shape=outs,
        in_specs=vmem(len(heads) + 1 + 2 * len(slabs)),
        out_specs=vmem(len(outs)),
        compiler_params=GRANT,
        cost_estimate=pl.CostEstimate(
            flops=(6 if stats else 4) * 2 * DOCS * K * SLAB * n,
            bytes_accessed=n << 20,
            transcendentals=2 * DOCS * SLAB * n,
        ),
    )(*heads, scale, *bs, *cs)


def plus(*terms):
    total = terms[0].astype(F32)
    for term in terms[1:]:
        total = total + term.astype(F32)
    return total.astype(BF16)


def scatter(s):
    down = lambda x: yfrom(x, 1)
    up = lambda x: yfrom(x, 3)
    x1 = xswap(s[2, 1, 0])
    u1 = down(s[2, 1, 1])
    x2 = xswap(s[1, 1, 0])
    d2 = up(s[1, 1, 1])
    u2 = down(plus(s[3, 1, 1], u1))
    x3 = xswap(s[3, 1, 0])
    d3 = up(s[2, 0, 1])
    mid = plus(s[2, 0, 0], x1)
    u3 = down(mid)
    u4 = down(s[3, 0, 1])
    x4 = xswap(plus(s[0, 1, 1], u2, d2))
    d4 = up(plus(s[1, 0, 0], x2))
    x5 = xswap(s[0, 1, 0])
    d5 = up(plus(s[1, 0, 1], d3))
    u5 = down(plus(s[3, 0, 0], x3, u3))
    return (s[0, 0, 0], x5, u5, d4), (s[0, 0, 1], x4, u4, d5)


def pseudo_kernel(*refs):
    halves = (refs[0:4], refs[4:8])
    x_ref, l_ref, total_ref, out = refs[8:12]
    total = total_ref[0:1, :]
    level = jnp.log((total + prior_count * V) / V)
    for h in range(2):
        for q in range(4):
            rows = slice(q * 256, (q + 1) * 256)
            acc = halves[h][0][:, rows].astype(F32)
            for ref in halves[h][1:]:
                acc = acc + ref[:, rows].astype(F32)
            x = x_ref[h * HALF + q * 256 : h * HALF + (q + 1) * 256, :]
            beta = jnp.exp(x - l_ref[0:1, :]).astype(BF16).astype(F32)
            out[4 * h + q, 0:256, :] = (jnp.log(beta * acc.T + prior_count) - level).astype(BF16)
    hi, mid, low = split3(total)
    row = lax.broadcasted_iota(jnp.int32, (16, K), 0)
    head = jnp.where(row == 0, hi.astype(F32), jnp.where(row == 1, mid.astype(F32), low.astype(F32)))
    for t in range(8):
        out[t, 256:272, :] = head.astype(BF16)


def pseudo_rows(half0, half1, x, level, total):
    return pl.pallas_call(
        pseudo_kernel,
        out_shape=jax.ShapeDtypeStruct((8, 272, K), BF16),
        in_specs=vmem(11),
        out_specs=pl.BlockSpec(memory_space=pltpu.VMEM),
        compiler_params=GRANT,
        name="pseudo_rows",
    )(*half0, *half1, x, level, total)


def smooth_kernel(y_ref, var_ref, noise_ref, out):
    var = var_ref[...]
    gains, factors = [], []
    previous = initial_scale * var
    for t in range(8):
        head = y_ref[t, 256:272, :].astype(F32)
        total = head[0:1] + head[1:2] + head[2:3]
        noise = noise_ref[...] * jnp.sum(total, axis=1, keepdims=True) / (K * total)
        predicted = previous + var
        gain = predicted / (predicted + noise)
        previous = (1.0 - gain) * predicted
        gains.append(gain)
        factors.append(previous / (previous + var))

    @pl.loop(0, 8)
    def _(i):
        rows = pl.ds(pl.multiple_of(i * 32, 32), 32)
        filtered = []
        value = None
        for t in range(8):
            new = gains[t] * y_ref[t, rows, :].astype(F32)
            value = new if t == 0 else (1.0 - gains[t]) * value + new
            filtered.append(value)
        out[7, rows, :] = value.astype(BF16)
        for t in range(6, -1, -1):
            value = (1.0 - factors[t]) * filtered[t] + factors[t] * value
            out[t, rows, :] = value.astype(BF16)


def smooth(y, var, noise):
    return pl.pallas_call(
        smooth_kernel,
        out_shape=jax.ShapeDtypeStruct((8, 256, K), BF16),
        in_specs=vmem(3),
        out_specs=pl.BlockSpec(memory_space=pltpu.VMEM),
        compiler_params=GRANT,
        name="smooth",
    )(y, var, noise)


def body(counts, topic_means, doc_topics_init, dirichlet_prior, chain_var, obs_noise):
    x = topic_means[0]
    y, xl, c = lax.axis_index("y"), lax.axis_index("xl"), lax.axis_index("c")
    chips = jnp.stack([lax.rem(y + dy, 4) * 2 + lax.rem(xl + dx, 2) for dy, dx in REL])
    counts = counts[0]
    init = doc_topics_init[0]

    b, b0, b1, level = slab_softmax(x)
    bx = xswap(b)
    u0, u1 = yfrom(b0, 3), yfrom(b1, 3)
    d0, d1 = yfrom(b0, 1), yfrom(b1, 1)
    other_init = across(init)
    theirs = across(counts)

    row = lax.broadcasted_iota(jnp.int32, (8, K), 0)
    pair = jnp.where(row % 2 == 0, level, jnp.logaddexp(level, across(level)))
    far = xswap(pair)
    levels = [jnp.where(row < 4, pair, far)]
    levels += [yfrom(levels[0], dy) for dy in (1, 2, 3)]

    x31, u20, d20 = xswap(u0), yfrom(u0, 3), yfrom(d1, 1)
    u31, d11 = yfrom(bx[HALF:], 3), yfrom(bx[HALF:], 1)
    x11 = xswap(d0)
    x21, u21 = xswap(u20), yfrom(u31, 3)

    index = {r: i for i, r in enumerate(REL)}
    orders = [[(0, 0), (0, 1), (3, 0), (1, 0)], [(2, 0), (3, 1), (1, 1)], [(2, 1)]]
    pieces = [(b, bx, u0, u1, d0, d1), (u20, d20, x31, u31, x11, d11), (x21, u21)]
    places = [
        [((0, 0), (0, HALF)), ((1, 0), (1, HALF)), ((2, 0), (3, 0)), ((4, 0), (5, 0))],
        [((0, 0), (1, 0)), ((2, 0), (3, 0)), ((4, 0), (5, 0))],
        [((0, 0), (1, 0))],
    ]
    slabs = tuple(tuple(index[r] for r in order) for order in orders)
    fetches = (slabs[0], slabs[1] + slabs[2], ())
    stay = lambda a: pltpu.with_memory_space_constraint(a, pltpu.HBM)
    heads = (stay(init), stay(other_init), *levels)
    given = (2 * chips + c, stay(counts), stay(theirs))
    bs, cs, parts = [], [], []
    for g in range(3):
        outs = first_sweep(
            slabs[g], fetches[g], places[g], heads, cs[1:] if g == 2 else given, pieces[g]
        )
        if g == 0:
            p, scale, whole, *outs = outs
            heads = (p, scale)
        parts.append(outs[0])
        bs.append(outs[1])
        cs.append(outs[2] if g < 2 else cs[1])
    part = parts[0] + parts[1] + parts[2]

    prior = dirichlet_prior[None, :]
    held = {(2, 1): (2, 0, HELD)}
    held.update({r: (g, i, i) for g in range(2) for i, r in enumerate(orders[g])})

    def swept(heads, wanted, stats=""):
        groups = sorted({held[r][0] for r in wanted}, reverse=True)
        slabs = tuple(
            tuple((index[r],) + held[r][1:] for r in wanted if held[r][0] == g) for g in groups
        )
        return sweep(heads, scale, slabs, [bs[g] for g in groups], [cs[g] for g in groups], stats)

    for _ in range(ITERS_E - 2):
        p, part = swept((part, across(part), p, prior), REL)

    stats = {}
    parts = []
    heads = (part, across(part), p, prior)
    for name, wanted in (
        ("stats_a", [(2, 1)]),
        ("stats_b", [(2, 0), (3, 1), (1, 1), (3, 0)]),
        ("stats_c", [(0, 0), (0, 1), (1, 0)]),
    ):
        outs = swept(heads, wanted, name)
        if not parts:
            p, *outs = outs
            heads = (p,)
        parts.append(outs[0])
        for j, r in enumerate(wanted):
            stats[r + (0,)], stats[r + (1,)] = outs[1 + 2 * j], outs[2 + 2 * j]
    part = parts[0] + parts[1] + parts[2]
    half0, half1 = scatter(stats)

    got = across(part)
    update = p.astype(F32) * (part + jnp.concatenate([got[DOCS:], got[:DOCS]], axis=0))
    concentration = prior + update[:DOCS]
    total = jnp.broadcast_to(jnp.sum(update, axis=0, keepdims=True), (8, K))
    total = total + xswap(total)
    total = total + yfrom(total, 3)
    total = total + yfrom(total, 2)

    rows = pseudo_rows(half0, half1, x, whole, total)
    rows = lax.all_to_all(rows, TM, 0, 0)
    smoothed = smooth(rows, chain_var[None, :], obs_noise[None, :])
    smoothed = lax.all_to_all(smoothed, TM, 0, 0)
    return smoothed.reshape(1, SLAB, K).astype(F32), concentration[None]


def solution(mesh):
    split = Mesh(mesh.devices.reshape(4, 2, 4, 2, 2), ("z", "xh", "y", "xl", "c"))
    docs = ("y", "xl", "c")
    placed = (P(TM, docs, None), P(TM, docs, None), P(TM, docs, None), P(), P(), P())

    return jax.shard_map(
        body,
        mesh=split,
        in_specs=placed,
        out_specs=(P(TM, docs, None), P(TM, docs, None)),
        check_vma=False,
    )
```

```python
import functools

import jax
import jax.numpy as jnp
from jax import lax
from jax.experimental import pallas as pl
from jax.experimental.pallas import tpu as pltpu
from jax.sharding import Mesh
from jax.sharding import PartitionSpec as P


V = 32768
K = 128
SLAB = 2048
HALF = 1024
HELD = 3
DOCS = 64
ITERS_E = 4
TM = ("z", "xh")

prior_count = 0.5
initial_scale = 1000.0

F32 = jnp.float32
BF16 = jnp.bfloat16
GRANT = pltpu.CompilerParams(vmem_limit_bytes=16 << 20)

REL = [(dy, dx) for dy in range(4) for dx in range(2)]


def across(x):
    return lax.ppermute(x, "c", [(0, 1), (1, 0)])


def xswap(x):
    return lax.ppermute(x, "xl", [(0, 1), (1, 0)])


def yfrom(x, dy):
    return lax.ppermute(x, "y", [((i + dy) % 4, i) for i in range(4)])


def vmem(n):
    return [pl.BlockSpec(memory_space=pltpu.VMEM)] * n


def split3(x):
    hi = x.astype(BF16)
    rest = x - hi.astype(F32)
    mid = rest.astype(BF16)
    low = (rest - mid.astype(F32)).astype(BF16)
    return hi, mid, low


def slab_kernel(hbm_ref, b_ref, b0_ref, b1_ref, l_ref, x_ref, e_ref, sem):
    copies = []
    for i in range(4):
        rows = pl.ds(i * 512, 512)
        copies.append(pltpu.make_async_copy(hbm_ref.at[rows], x_ref.at[rows], sem.at[i]))
        copies[-1].start()
    m8 = jnp.full((8, K), -jnp.inf, F32)
    for i in range(4):
        copies[i].wait()
        block = x_ref[i * 512 : (i + 1) * 512, :].reshape(64, 8, K)
        m8 = jnp.maximum(m8, jnp.max(block, axis=0))
    m = jnp.max(m8, axis=0, keepdims=True)

    def mass(i, s):
        e = jnp.exp(x_ref[pl.ds(i * 256, 256), :] - m)
        e_ref[pl.ds(i * 256, 256), :] = e
        return s + jnp.sum(e.reshape(32, 8, K), axis=0)

    s8 = lax.fori_loop(0, 8, mass, jnp.zeros((8, K), F32))
    s = jnp.sum(s8, axis=0, keepdims=True)
    inverse = 1.0 / s
    l_ref[...] = jnp.broadcast_to(m + jnp.log(s), (8, K))

    for h, half in enumerate((b0_ref, b1_ref)):

        @pl.loop(0, 4)
        def _(i, h=h, half=half):
            rows = pl.ds(pl.multiple_of(h * HALF + i * 256, 256), 256)
            beta = (e_ref[rows, :] * inverse).astype(BF16)
            b_ref[rows, :] = beta
            half[pl.ds(pl.multiple_of(i * 256, 256), 256), :] = beta


def slab_softmax(x):
    return pl.pallas_call(
        slab_kernel,
        out_shape=(
            jax.ShapeDtypeStruct((SLAB, K), BF16),
            jax.ShapeDtypeStruct((HALF, K), BF16),
            jax.ShapeDtypeStruct((HALF, K), BF16),
            jax.ShapeDtypeStruct((8, K), F32),
        ),
        in_specs=[pl.BlockSpec(memory_space=pl.ANY)],
        out_specs=tuple(vmem(4)),
        scratch_shapes=[pltpu.VMEM((SLAB, K), F32)] * 2 + [pltpu.SemaphoreType.DMA((4,))],
        compiler_params=GRANT,
        name="slab_softmax",
    )(pltpu.with_memory_space_constraint(x, pltpu.HBM))


def digamma(x):
    total = jnp.zeros_like(x)
    for i in range(8):
        total = total + 1.0 / (x + float(i))
    y = x + 8.0
    r = 1.0 / y
    r2 = r * r
    tail = r2 * (1.0 / 12.0 - r2 * (1.0 / 120.0 - r2 * (1.0 / 252.0 - r2 * (1.0 / 240.0))))
    return jnp.log(y) - 0.5 * r - tail - total


def words_of(scaled, beta, count):
    mix = lax.dot_general(scaled, beta, (((1,), (1,)), ((), ())), preferred_element_type=F32)
    return (count.astype(F32) / mix).astype(BF16)


def first_kernel(slabs, fetch, places, n_in, lead, *refs):
    n = len(slabs)
    refs = list(refs)
    if lead:
        inits, levels = refs[:2], refs[2:6]
        refs = refs[6:]
    else:
        given, scale_ref = refs[:2]
        refs = refs[2:]
    if fetch:
        at_ref, counts, theirs = refs[:3]
        refs = refs[3:]
    else:
        cs, refs = refs[0].at[pl.ds(HELD, 1)], refs[1:]
    b_in = refs[:n_in]
    refs = refs[n_in:]
    if lead:
        p_out, scale_out, whole_out = refs[:3]
        refs = refs[3:]
    part, bs = refs[:2]
    if fetch:
        cs, raw, sem_r = refs[2:5]
        refs = refs[3:]
    sem_b = refs[2]

    if lead:
        gamma, sem_g = refs[3:]
        starts = [
            pltpu.make_async_copy(ref, gamma.at[pl.ds(side * DOCS, DOCS)], sem_g.at[side])
            for side, ref in enumerate(inits)
        ]
        for copy in starts:
            copy.start()

    copies = []
    for i, r in enumerate(slabs):
        group = []
        for h in range(2):
            source, row = places[i][h]
            group.append(
                pltpu.make_async_copy(
                    b_in[source].at[pl.ds(row, HALF)], bs.at[i, pl.ds(h * HALF, HALF)], sem_b.at[i, h]
                )
            )
        copies.append(group)
    for i, r in enumerate(fetch):
        if i >= n:
            copies.append([])
        words = pl.ds(pl.multiple_of(at_ref[r] * SLAB, SLAB), SLAB)
        for side, ref in enumerate((counts, theirs)):
            copies[i].append(
                pltpu.make_async_copy(
                    ref.at[:, words], raw.at[i, pl.ds(side * DOCS, DOCS)], sem_r.at[i, side]
                )
            )
    for group in copies:
        for copy in group:
            copy.start()

    if lead:
        chips = [levels[dy][4 * dx + 1 : 4 * dx + 2, :] for dy, dx in REL]
        peak = functools.reduce(jnp.maximum, chips)
        mass = functools.reduce(jnp.add, [jnp.exp(chip - peak) for chip in chips])
        whole = peak + jnp.log(mass)
        whole_out[...] = jnp.broadcast_to(whole, (8, K))
        rows = [jnp.exp(levels[dy][4 * dx : 4 * dx + 1, :] - whole) for dy, dx in REL]
        for r in range(8):
            scale_out[r : r + 1, :] = rows[r]
        for copy in starts:
            copy.wait()
        p = jnp.exp(digamma(gamma[...])).astype(BF16)
        p_out[...] = p
    else:
        p = given[...]
        rows = [scale_ref[r : r + 1, :] for r in range(8)]
    p32 = p.astype(F32)

    total = jnp.zeros((2 * DOCS, K), F32)
    for i, r in enumerate(slabs):
        for copy in copies[i]:
            copy.wait()
        if fetch:
            cs[i] = raw[i].astype(F32).astype(BF16)
        ratio = words_of((p32 * rows[r]).astype(BF16), bs[i], cs[i])
        total = total + jnp.dot(ratio, bs[i], preferred_element_type=F32) * rows[r]
    part[...] = total
    for i in range(n, len(fetch)):
        for copy in copies[i]:
            copy.wait()
        cs[i] = raw[i].astype(F32).astype(BF16)


def first_sweep(slabs, fetch, places, heads, counts, pieces):
    n, lead = len(slabs), len(heads) == 6
    outs = []
    if lead:
        outs.append(jax.ShapeDtypeStruct((2 * DOCS, K), BF16))
        outs += [jax.ShapeDtypeStruct((8, K), F32)] * 2
    outs.append(jax.ShapeDtypeStruct((2 * DOCS, K), F32))
    outs.append(jax.ShapeDtypeStruct((n, SLAB, K), BF16))
    if fetch:
        outs.append(jax.ShapeDtypeStruct((len(fetch), 2 * DOCS, SLAB), BF16))
    anywhere = [pl.BlockSpec(memory_space=pl.ANY)]
    return pl.pallas_call(
        functools.partial(first_kernel, slabs, fetch, places, len(pieces), lead),
        out_shape=outs,
        in_specs=(anywhere * 2 + vmem(4) if lead else vmem(2))
        + ([pl.BlockSpec(memory_space=pltpu.SMEM)] + anywhere * 2 if fetch else vmem(1))
        + anywhere * len(pieces),
        out_specs=vmem(len(outs)),
        scratch_shapes=[
            pltpu.VMEM((len(fetch), 2 * DOCS, SLAB), jnp.int32),
            pltpu.SemaphoreType.DMA((len(fetch), 2)),
        ][: 2 if fetch else 0]
        + [pltpu.SemaphoreType.DMA((n, 2))]
        + ([pltpu.VMEM((2 * DOCS, K), F32), pltpu.SemaphoreType.DMA((2,))] if lead else []),
        compiler_params=GRANT,
        cost_estimate=pl.CostEstimate(
            flops=4 * 2 * DOCS * K * SLAB * n,
            bytes_accessed=2 * n << 20,
            transcendentals=2 * DOCS * SLAB * n,
        ),
    )(*heads, *counts, *pieces)


def sweep_kernel(heads, slabs, stats, *refs):
    groups, lead = len(slabs), heads > 1
    refs = list(refs)
    head, scale, refs = refs[:heads], refs[heads], refs[heads + 1 :]
    bs, cs = refs[:groups], refs[groups : 2 * groups]
    refs = refs[2 * groups :]
    if lead:
        mine, got, before, prior = head
        got = got[...]
        total = mine[...] + jnp.concatenate([got[DOCS:], got[:DOCS]], axis=0)
        gamma = prior[...] + before[...].astype(F32) * total
        p = jnp.exp(digamma(gamma)).astype(BF16)
        refs.pop(0)[...] = p
    else:
        p = head[0][...]
    part = refs.pop(0)
    p32 = p.astype(F32)
    if stats:
        pt = p32.T.astype(BF16)

    steps = [(g, i, h) for g in range(groups) for i in range(len(slabs[g])) for h in range(2)]

    def mixture(g, i, h):
        r, at_b, _ = slabs[g][i]
        scaled = (p32 * scale[r : r + 1, :]).astype(BF16)
        return lax.dot_general(
            scaled,
            bs[g][at_b, h * HALF : (h + 1) * HALF, :],
            (((1,), (1,)), ((), ())),
            preferred_element_type=F32,
        )

    total = jnp.zeros((2 * DOCS, K), F32)
    ahead = mixture(*steps[0])
    for at, (g, i, h) in enumerate(steps):
        mix = ahead
        if at + 1 < len(steps):
            ahead = mixture(*steps[at + 1])
        r, at_b, at_c = slabs[g][i]
        words = slice(h * HALF, (h + 1) * HALF)
        ratio = (cs[g][at_c, :, words].astype(F32) / mix).astype(BF16)
        new = jnp.dot(ratio, bs[g][at_b, words, :], preferred_element_type=F32)
        acc = new if h == 0 else acc + new
        if h == 1:
            total = total + acc * scale[r : r + 1, :]
        if stats:
            refs[at][...] = jnp.dot(pt, ratio, preferred_element_type=F32).astype(BF16)
    part[...] = total


def sweep(heads, scale, slabs, bs, cs, stats=""):
    n = sum(len(group) for group in slabs)
    lead = len(heads) > 1
    outs = []
    if lead:
        outs.append(jax.ShapeDtypeStruct((2 * DOCS, K), BF16))
    outs.append(jax.ShapeDtypeStruct((2 * DOCS, K), F32))
    if stats:
        outs += [jax.ShapeDtypeStruct((K, HALF), BF16)] * (2 * n)
    return pl.pallas_call(
        functools.partial(sweep_kernel, len(heads), slabs, bool(stats)),
        out_shape=outs,
        in_specs=vmem(len(heads) + 1 + 2 * len(slabs)),
        out_specs=vmem(len(outs)),
        compiler_params=GRANT,
        cost_estimate=pl.CostEstimate(
            flops=(6 if stats else 4) * 2 * DOCS * K * SLAB * n,
            bytes_accessed=n << 20,
            transcendentals=2 * DOCS * SLAB * n,
        ),
    )(*heads, scale, *bs, *cs)


def plus(*terms):
    total = terms[0].astype(F32)
    for term in terms[1:]:
        total = total + term.astype(F32)
    return total.astype(BF16)


def scatter(s):
    down = lambda x: yfrom(x, 1)
    up = lambda x: yfrom(x, 3)
    x1 = xswap(s[2, 1, 0])
    u1 = down(s[2, 1, 1])
    x2 = xswap(s[1, 1, 0])
    d2 = up(s[1, 1, 1])
    u2 = down(plus(s[3, 1, 1], u1))
    x3 = xswap(s[3, 1, 0])
    d3 = up(s[2, 0, 1])
    u3 = down(plus(s[2, 0, 0], x1))
    u4 = down(s[3, 0, 1])
    x4 = xswap(plus(s[0, 1, 1], u2, d2))
    d4 = up(plus(s[1, 0, 0], x2))
    x5 = xswap(s[0, 1, 0])
    d5 = up(plus(s[1, 0, 1], d3))
    u5 = down(plus(s[3, 0, 0], x3, u3))
    return (s[0, 0, 0], x5, u5, d4), (s[0, 0, 1], x4, u4, d5)


def pseudo_kernel(*refs):
    halves = (refs[0:4], refs[4:8])
    x_ref, l_ref, total_ref, out = refs[8:12]
    total = total_ref[0:1, :]
    level = jnp.log((total + prior_count * V) / V)
    for h in range(2):
        for q in range(4):
            rows = slice(q * 256, (q + 1) * 256)
            acc = halves[h][0][:, rows].astype(F32)
            for ref in halves[h][1:]:
                acc = acc + ref[:, rows].astype(F32)
            x = x_ref[h * HALF + q * 256 : h * HALF + (q + 1) * 256, :]
            beta = jnp.exp(x - l_ref[0:1, :]).astype(BF16).astype(F32)
            out[4 * h + q, 0:256, :] = (jnp.log(beta * acc.T + prior_count) - level).astype(BF16)
    hi, mid, low = split3(total)
    row = lax.broadcasted_iota(jnp.int32, (16, K), 0)
    head = jnp.where(row == 0, hi.astype(F32), jnp.where(row == 1, mid.astype(F32), low.astype(F32)))
    for t in range(8):
        out[t, 256:272, :] = head.astype(BF16)


def pseudo_rows(half0, half1, x, level, total):
    return pl.pallas_call(
        pseudo_kernel,
        out_shape=jax.ShapeDtypeStruct((8, 272, K), BF16),
        in_specs=vmem(11),
        out_specs=pl.BlockSpec(memory_space=pltpu.VMEM),
        compiler_params=GRANT,
        name="pseudo_rows",
    )(*half0, *half1, x, level, total)


def smooth_kernel(y_ref, var_ref, noise_ref, out):
    var = var_ref[...]
    gains, factors = [], []
    previous = initial_scale * var
    for t in range(8):
        head = y_ref[t, 256:272, :].astype(F32)
        total = head[0:1] + head[1:2] + head[2:3]
        noise = noise_ref[...] * jnp.sum(total, axis=1, keepdims=True) / (K * total)
        predicted = previous + var
        gain = predicted / (predicted + noise)
        previous = (1.0 - gain) * predicted
        gains.append(gain)
        factors.append(previous / (previous + var))

    @pl.loop(0, 8, unroll=4)
    def _(i):
        rows = pl.ds(pl.multiple_of(i * 32, 32), 32)
        filtered = []
        value = None
        for t in range(8):
            new = gains[t] * y_ref[t, rows, :].astype(F32)
            value = new if t == 0 else (1.0 - gains[t]) * value + new
            filtered.append(value)
        out[7, rows, :] = value.astype(BF16)
        for t in range(6, -1, -1):
            value = (1.0 - factors[t]) * filtered[t] + factors[t] * value
            out[t, rows, :] = value.astype(BF16)


def smooth(y, var, noise):
    return pl.pallas_call(
        smooth_kernel,
        out_shape=jax.ShapeDtypeStruct((8, 256, K), BF16),
        in_specs=vmem(3),
        out_specs=pl.BlockSpec(memory_space=pltpu.VMEM),
        compiler_params=GRANT,
        name="smooth",
    )(y, var, noise)


def body(counts, topic_means, doc_topics_init, dirichlet_prior, chain_var, obs_noise):
    x = topic_means[0]
    y, xl, c = lax.axis_index("y"), lax.axis_index("xl"), lax.axis_index("c")
    chips = jnp.stack([lax.rem(y + dy, 4) * 2 + lax.rem(xl + dx, 2) for dy, dx in REL])
    counts = counts[0]
    init = doc_topics_init[0]

    b, b0, b1, level = slab_softmax(x)
    bx = xswap(b)
    u0, u1 = yfrom(b0, 3), yfrom(b1, 3)
    d0, d1 = yfrom(b0, 1), yfrom(b1, 1)
    other_init = across(init)
    theirs = across(counts)

    row = lax.broadcasted_iota(jnp.int32, (8, K), 0)
    pair = jnp.where(row % 2 == 0, level, jnp.logaddexp(level, across(level)))
    far = xswap(pair)
    levels = [jnp.where(row < 4, pair, far)]
    levels += [yfrom(levels[0], dy) for dy in (1, 2, 3)]

    x31, u20, d20 = xswap(u0), yfrom(u0, 3), yfrom(d1, 1)
    u31, d11 = yfrom(bx[HALF:], 3), yfrom(bx[HALF:], 1)
    x11 = xswap(d0)
    x21, u21 = xswap(u20), yfrom(u31, 3)

    index = {r: i for i, r in enumerate(REL)}
    orders = [[(0, 0), (0, 1), (3, 0), (1, 0)], [(2, 0), (3, 1), (1, 1)], [(2, 1)]]
    pieces = [(b, bx, u0, u1, d0, d1), (u20, d20, x31, u31, x11, d11), (x21, u21)]
    places = [
        [((0, 0), (0, HALF)), ((1, 0), (1, HALF)), ((2, 0), (3, 0)), ((4, 0), (5, 0))],
        [((0, 0), (1, 0)), ((2, 0), (3, 0)), ((4, 0), (5, 0))],
        [((0, 0), (1, 0))],
    ]
    slabs = tuple(tuple(index[r] for r in order) for order in orders)
    fetches = (slabs[0], slabs[1] + slabs[2], ())
    stay = lambda a: pltpu.with_memory_space_constraint(a, pltpu.HBM)
    heads = (stay(init), stay(other_init), *levels)
    given = (2 * chips + c, stay(counts), stay(theirs))
    bs, cs, parts = [], [], []
    for g in range(3):
        outs = first_sweep(
            slabs[g], fetches[g], places[g], heads, cs[1:] if g == 2 else given, pieces[g]
        )
        if g == 0:
            p, scale, whole, *outs = outs
            heads = (p, scale)
        parts.append(outs[0])
        bs.append(outs[1])
        cs.append(outs[2] if g < 2 else cs[1])
    part = parts[0] + parts[1] + parts[2]

    prior = dirichlet_prior[None, :]
    held = {(2, 1): (2, 0, HELD)}
    held.update({r: (g, i, i) for g in range(2) for i, r in enumerate(orders[g])})

    def swept(heads, wanted, stats=""):
        groups = sorted({held[r][0] for r in wanted}, reverse=True)
        slabs = tuple(
            tuple((index[r],) + held[r][1:] for r in wanted if held[r][0] == g) for g in groups
        )
        return sweep(heads, scale, slabs, [bs[g] for g in groups], [cs[g] for g in groups], stats)

    for _ in range(ITERS_E - 2):
        p, part = swept((part, across(part), p, prior), REL)

    stats = {}
    parts = []
    heads = (part, across(part), p, prior)
    for name, wanted in (
        ("stats_a", [(2, 1)]),
        ("stats_b", [(2, 0), (3, 1), (1, 1), (3, 0)]),
        ("stats_c", [(0, 0), (0, 1), (1, 0)]),
    ):
        outs = swept(heads, wanted, name)
        if not parts:
            p, *outs = outs
            heads = (p,)
        parts.append(outs[0])
        for j, r in enumerate(wanted):
            stats[r + (0,)], stats[r + (1,)] = outs[1 + 2 * j], outs[2 + 2 * j]
    part = parts[0] + parts[1] + parts[2]
    half0, half1 = scatter(stats)

    got = across(part)
    update = p.astype(F32) * (part + jnp.concatenate([got[DOCS:], got[:DOCS]], axis=0))
    concentration = prior + update[:DOCS]
    total = jnp.broadcast_to(jnp.sum(update, axis=0, keepdims=True), (8, K))
    total = total + xswap(total)
    total = total + yfrom(total, 3)
    total = total + yfrom(total, 2)

    rows = pseudo_rows(half0, half1, x, whole, total)
    rows = lax.all_to_all(rows, TM, 0, 0)
    smoothed = smooth(rows, chain_var[None, :], obs_noise[None, :])
    smoothed = lax.all_to_all(smoothed, TM, 0, 0)
    return smoothed.reshape(1, SLAB, K).astype(F32), concentration[None]


def solution(mesh):
    split = Mesh(mesh.devices.reshape(4, 2, 4, 2, 2), ("z", "xh", "y", "xl", "c"))
    docs = ("y", "xl", "c")
    placed = (P(TM, docs, None), P(TM, docs, None), P(TM, docs, None), P(), P(), P())

    return jax.shard_map(
        body,
        mesh=split,
        in_specs=placed,
        out_specs=(P(TM, docs, None), P(TM, docs, None)),
        check_vma=False,
    )
```

```python
import functools

import jax
import jax.numpy as jnp
from jax import lax
from jax.experimental import pallas as pl
from jax.experimental.pallas import tpu as pltpu
from jax.sharding import Mesh
from jax.sharding import PartitionSpec as P


V = 32768
K = 128
SLAB = 2048
HALF = 1024
HELD = 3
DOCS = 64
ITERS_E = 4
TM = ("z", "xh")

prior_count = 0.5
initial_scale = 1000.0

F32 = jnp.float32
BF16 = jnp.bfloat16
GRANT = pltpu.CompilerParams(vmem_limit_bytes=16 << 20)

REL = [(dy, dx) for dy in range(4) for dx in range(2)]


def across(x):
    return lax.ppermute(x, "c", [(0, 1), (1, 0)])


def xswap(x):
    return lax.ppermute(x, "xl", [(0, 1), (1, 0)])


def yfrom(x, dy):
    return lax.ppermute(x, "y", [((i + dy) % 4, i) for i in range(4)])


def vmem(n):
    return [pl.BlockSpec(memory_space=pltpu.VMEM)] * n


def split3(x):
    hi = x.astype(BF16)
    rest = x - hi.astype(F32)
    mid = rest.astype(BF16)
    low = (rest - mid.astype(F32)).astype(BF16)
    return hi, mid, low


def slab_kernel(hbm_ref, b_ref, b0_ref, b1_ref, l_ref, x_ref, e_ref, sem):
    copies = []
    for i in range(4):
        rows = pl.ds(i * 512, 512)
        copies.append(pltpu.make_async_copy(hbm_ref.at[rows], x_ref.at[rows], sem.at[i]))
        copies[-1].start()
    m8 = jnp.full((8, K), -jnp.inf, F32)
    for i in range(4):
        copies[i].wait()
        block = x_ref[i * 512 : (i + 1) * 512, :].reshape(64, 8, K)
        m8 = jnp.maximum(m8, jnp.max(block, axis=0))
    m = jnp.max(m8, axis=0, keepdims=True)

    def mass(i, s):
        e = jnp.exp(x_ref[pl.ds(i * 256, 256), :] - m)
        e_ref[pl.ds(i * 256, 256), :] = e
        return s + jnp.sum(e.reshape(32, 8, K), axis=0)

    s8 = lax.fori_loop(0, 8, mass, jnp.zeros((8, K), F32))
    s = jnp.sum(s8, axis=0, keepdims=True)
    inverse = 1.0 / s
    l_ref[...] = jnp.broadcast_to(m + jnp.log(s), (8, K))

    for h, half in enumerate((b0_ref, b1_ref)):

        @pl.loop(0, 4)
        def _(i, h=h, half=half):
            rows = pl.ds(pl.multiple_of(h * HALF + i * 256, 256), 256)
            beta = (e_ref[rows, :] * inverse).astype(BF16)
            b_ref[rows, :] = beta
            half[pl.ds(pl.multiple_of(i * 256, 256), 256), :] = beta


def slab_softmax(x):
    return pl.pallas_call(
        slab_kernel,
        out_shape=(
            jax.ShapeDtypeStruct((SLAB, K), BF16),
            jax.ShapeDtypeStruct((HALF, K), BF16),
            jax.ShapeDtypeStruct((HALF, K), BF16),
            jax.ShapeDtypeStruct((8, K), F32),
        ),
        in_specs=[pl.BlockSpec(memory_space=pl.ANY)],
        out_specs=tuple(vmem(4)),
        scratch_shapes=[pltpu.VMEM((SLAB, K), F32)] * 2 + [pltpu.SemaphoreType.DMA((4,))],
        compiler_params=GRANT,
        name="slab_softmax",
    )(pltpu.with_memory_space_constraint(x, pltpu.HBM))


def digamma(x):
    total = jnp.zeros_like(x)
    for i in range(0, 8, 2):
        a, b = x + float(i), x + float(i + 1)
        total = total + (a + b) / (a * b)
    y = x + 8.0
    r = 1.0 / y
    r2 = r * r
    tail = r2 * (1.0 / 12.0 - r2 * (1.0 / 120.0 - r2 * (1.0 / 252.0 - r2 * (1.0 / 240.0))))
    return jnp.log(y) - 0.5 * r - tail - total


def words_of(scaled, beta, count):
    mix = lax.dot_general(scaled, beta, (((1,), (1,)), ((), ())), preferred_element_type=F32)
    return (count.astype(F32) / mix).astype(BF16)


def first_kernel(slabs, fetch, places, n_in, lead, *refs):
    n = len(slabs)
    refs = list(refs)
    if lead:
        inits, levels = refs[:2], refs[2:6]
        refs = refs[6:]
    else:
        given, scale_ref = refs[:2]
        refs = refs[2:]
    if fetch:
        at_ref, counts, theirs = refs[:3]
        refs = refs[3:]
    else:
        cs, refs = refs[0].at[pl.ds(HELD, 1)], refs[1:]
    b_in = refs[:n_in]
    refs = refs[n_in:]
    if lead:
        p_out, scale_out, whole_out = refs[:3]
        refs = refs[3:]
    part, bs = refs[:2]
    if fetch:
        cs, raw, sem_r = refs[2:5]
        refs = refs[3:]
    sem_b = refs[2]

    if lead:
        gamma, sem_g = refs[3:]
        starts = [
            pltpu.make_async_copy(ref, gamma.at[pl.ds(side * DOCS, DOCS)], sem_g.at[side])
            for side, ref in enumerate(inits)
        ]
        for copy in starts:
            copy.start()

    copies = []
    for i, r in enumerate(slabs):
        group = []
        for h in range(2):
            source, row = places[i][h]
            group.append(
                pltpu.make_async_copy(
                    b_in[source].at[pl.ds(row, HALF)], bs.at[i, pl.ds(h * HALF, HALF)], sem_b.at[i, h]
                )
            )
        copies.append(group)
    for i, r in enumerate(fetch):
        if i >= n:
            copies.append([])
        words = pl.ds(pl.multiple_of(at_ref[r] * SLAB, SLAB), SLAB)
        for side, ref in enumerate((counts, theirs)):
            copies[i].append(
                pltpu.make_async_copy(
                    ref.at[:, words], raw.at[i, pl.ds(side * DOCS, DOCS)], sem_r.at[i, side]
                )
            )
    for group in copies:
        for copy in group:
            copy.start()

    if lead:
        chips = [levels[dy][4 * dx + 1 : 4 * dx + 2, :] for dy, dx in REL]
        peak = functools.reduce(jnp.maximum, chips)
        mass = functools.reduce(jnp.add, [jnp.exp(chip - peak) for chip in chips])
        whole = peak + jnp.log(mass)
        whole_out[...] = jnp.broadcast_to(whole, (8, K))
        rows = [jnp.exp(levels[dy][4 * dx : 4 * dx + 1, :] - whole) for dy, dx in REL]
        for r in range(8):
            scale_out[r : r + 1, :] = rows[r]
        for copy in starts:
            copy.wait()
        p = jnp.exp(digamma(gamma[...])).astype(BF16)
        p_out[...] = p
    else:
        p = given[...]
        rows = [scale_ref[r : r + 1, :] for r in range(8)]
    p32 = p.astype(F32)

    total = jnp.zeros((2 * DOCS, K), F32)
    for i, r in enumerate(slabs):
        for copy in copies[i]:
            copy.wait()
        if fetch:
            cs[i] = raw[i].astype(F32).astype(BF16)
        ratio = words_of((p32 * rows[r]).astype(BF16), bs[i], cs[i])
        total = total + jnp.dot(ratio, bs[i], preferred_element_type=F32) * rows[r]
    part[...] = total
    for i in range(n, len(fetch)):
        for copy in copies[i]:
            copy.wait()
        cs[i] = raw[i].astype(F32).astype(BF16)


def first_sweep(slabs, fetch, places, heads, counts, pieces):
    n, lead = len(slabs), len(heads) == 6
    outs = []
    if lead:
        outs.append(jax.ShapeDtypeStruct((2 * DOCS, K), BF16))
        outs += [jax.ShapeDtypeStruct((8, K), F32)] * 2
    outs.append(jax.ShapeDtypeStruct((2 * DOCS, K), F32))
    outs.append(jax.ShapeDtypeStruct((n, SLAB, K), BF16))
    if fetch:
        outs.append(jax.ShapeDtypeStruct((len(fetch), 2 * DOCS, SLAB), BF16))
    anywhere = [pl.BlockSpec(memory_space=pl.ANY)]
    return pl.pallas_call(
        functools.partial(first_kernel, slabs, fetch, places, len(pieces), lead),
        out_shape=outs,
        in_specs=(anywhere * 2 + vmem(4) if lead else vmem(2))
        + ([pl.BlockSpec(memory_space=pltpu.SMEM)] + anywhere * 2 if fetch else vmem(1))
        + anywhere * len(pieces),
        out_specs=vmem(len(outs)),
        scratch_shapes=[
            pltpu.VMEM((len(fetch), 2 * DOCS, SLAB), jnp.int32),
            pltpu.SemaphoreType.DMA((len(fetch), 2)),
        ][: 2 if fetch else 0]
        + [pltpu.SemaphoreType.DMA((n, 2))]
        + ([pltpu.VMEM((2 * DOCS, K), F32), pltpu.SemaphoreType.DMA((2,))] if lead else []),
        compiler_params=GRANT,
        cost_estimate=pl.CostEstimate(
            flops=4 * 2 * DOCS * K * SLAB * n,
            bytes_accessed=2 * n << 20,
            transcendentals=2 * DOCS * SLAB * n,
        ),
    )(*heads, *counts, *pieces)


def sweep_kernel(heads, slabs, stats, *refs):
    groups, lead = len(slabs), heads > 1
    refs = list(refs)
    head, scale, refs = refs[:heads], refs[heads], refs[heads + 1 :]
    bs, cs = refs[:groups], refs[groups : 2 * groups]
    refs = refs[2 * groups :]
    if lead:
        mine, got, before, prior = head
        got = got[...]
        total = mine[...] + jnp.concatenate([got[DOCS:], got[:DOCS]], axis=0)
        gamma = prior[...] + before[...].astype(F32) * total
        p = jnp.exp(digamma(gamma)).astype(BF16)
        refs.pop(0)[...] = p
    else:
        p = head[0][...]
    part = refs.pop(0)
    p32 = p.astype(F32)
    if stats:
        pt = p32.T.astype(BF16)

    steps = [(g, i, h) for g in range(groups) for i in range(len(slabs[g])) for h in range(2)]

    def mixture(g, i, h):
        r, at_b, _ = slabs[g][i]
        scaled = (p32 * scale[r : r + 1, :]).astype(BF16)
        return lax.dot_general(
            scaled,
            bs[g][at_b, h * HALF : (h + 1) * HALF, :],
            (((1,), (1,)), ((), ())),
            preferred_element_type=F32,
        )

    total = jnp.zeros((2 * DOCS, K), F32)
    ahead = mixture(*steps[0])
    for at, (g, i, h) in enumerate(steps):
        mix = ahead
        if at + 1 < len(steps):
            ahead = mixture(*steps[at + 1])
        r, at_b, at_c = slabs[g][i]
        words = slice(h * HALF, (h + 1) * HALF)
        ratio = (cs[g][at_c, :, words].astype(F32) / mix).astype(BF16)
        new = jnp.dot(ratio, bs[g][at_b, words, :], preferred_element_type=F32)
        acc = new if h == 0 else acc + new
        if h == 1:
            total = total + acc * scale[r : r + 1, :]
        if stats:
            refs[at][...] = jnp.dot(pt, ratio, preferred_element_type=F32).astype(BF16)
    part[...] = total


def sweep(heads, scale, slabs, bs, cs, stats=""):
    n = sum(len(group) for group in slabs)
    lead = len(heads) > 1
    outs = []
    if lead:
        outs.append(jax.ShapeDtypeStruct((2 * DOCS, K), BF16))
    outs.append(jax.ShapeDtypeStruct((2 * DOCS, K), F32))
    if stats:
        outs += [jax.ShapeDtypeStruct((K, HALF), BF16)] * (2 * n)
    return pl.pallas_call(
        functools.partial(sweep_kernel, len(heads), slabs, bool(stats)),
        out_shape=outs,
        in_specs=vmem(len(heads) + 1 + 2 * len(slabs)),
        out_specs=vmem(len(outs)),
        compiler_params=GRANT,
        cost_estimate=pl.CostEstimate(
            flops=(6 if stats else 4) * 2 * DOCS * K * SLAB * n,
            bytes_accessed=n << 20,
            transcendentals=2 * DOCS * SLAB * n,
        ),
    )(*heads, scale, *bs, *cs)


def plus(*terms):
    total = terms[0].astype(F32)
    for term in terms[1:]:
        total = total + term.astype(F32)
    return total.astype(BF16)


def scatter(s):
    down = lambda x: yfrom(x, 1)
    up = lambda x: yfrom(x, 3)
    x1 = xswap(s[2, 1, 0])
    u1 = down(s[2, 1, 1])
    x2 = xswap(s[1, 1, 0])
    d2 = up(s[1, 1, 1])
    u2 = down(plus(s[3, 1, 1], u1))
    x3 = xswap(s[3, 1, 0])
    d3 = up(s[2, 0, 1])
    u3 = down(plus(s[2, 0, 0], x1))
    u4 = down(s[3, 0, 1])
    x4 = xswap(plus(s[0, 1, 1], u2, d2))
    d4 = up(plus(s[1, 0, 0], x2))
    x5 = xswap(s[0, 1, 0])
    d5 = up(plus(s[1, 0, 1], d3))
    u5 = down(plus(s[3, 0, 0], x3, u3))
    return (s[0, 0, 0], x5, u5, d4), (s[0, 0, 1], x4, u4, d5)


def pseudo_kernel(*refs):
    halves = (refs[0:4], refs[4:8])
    x_ref, l_ref, total_ref, out = refs[8:12]
    total = total_ref[0:1, :]
    level = jnp.log((total + prior_count * V) / V)
    for h in range(2):
        for q in range(4):
            rows = slice(q * 256, (q + 1) * 256)
            acc = halves[h][0][:, rows].astype(F32)
            for ref in halves[h][1:]:
                acc = acc + ref[:, rows].astype(F32)
            x = x_ref[h * HALF + q * 256 : h * HALF + (q + 1) * 256, :]
            beta = jnp.exp(x - l_ref[0:1, :]).astype(BF16).astype(F32)
            out[4 * h + q, 0:256, :] = (jnp.log(beta * acc.T + prior_count) - level).astype(BF16)
    hi, mid, low = split3(total)
    row = lax.broadcasted_iota(jnp.int32, (16, K), 0)
    head = jnp.where(row == 0, hi.astype(F32), jnp.where(row == 1, mid.astype(F32), low.astype(F32)))
    for t in range(8):
        out[t, 256:272, :] = head.astype(BF16)


def pseudo_rows(half0, half1, x, level, total):
    return pl.pallas_call(
        pseudo_kernel,
        out_shape=jax.ShapeDtypeStruct((8, 272, K), BF16),
        in_specs=vmem(11),
        out_specs=pl.BlockSpec(memory_space=pltpu.VMEM),
        compiler_params=GRANT,
        name="pseudo_rows",
    )(*half0, *half1, x, level, total)


def smooth_kernel(y_ref, var_ref, noise_ref, out):
    var = var_ref[...]
    gains, factors = [], []
    previous = initial_scale * var
    for t in range(8):
        head = y_ref[t, 256:272, :].astype(F32)
        total = head[0:1] + head[1:2] + head[2:3]
        noise = noise_ref[...] * jnp.sum(total, axis=1, keepdims=True) / (K * total)
        predicted = previous + var
        gain = predicted / (predicted + noise)
        previous = (1.0 - gain) * predicted
        gains.append(gain)
        factors.append(previous / (previous + var))

    @pl.loop(0, 8, unroll=4)
    def _(i):
        rows = pl.ds(pl.multiple_of(i * 32, 32), 32)
        filtered = []
        value = None
        for t in range(8):
            new = gains[t] * y_ref[t, rows, :].astype(F32)
            value = new if t == 0 else (1.0 - gains[t]) * value + new
            filtered.append(value)
        out[7, rows, :] = value.astype(BF16)
        for t in range(6, -1, -1):
            value = (1.0 - factors[t]) * filtered[t] + factors[t] * value
            out[t, rows, :] = value.astype(BF16)


def smooth(y, var, noise):
    return pl.pallas_call(
        smooth_kernel,
        out_shape=jax.ShapeDtypeStruct((8, 256, K), BF16),
        in_specs=vmem(3),
        out_specs=pl.BlockSpec(memory_space=pltpu.VMEM),
        compiler_params=GRANT,
        name="smooth",
    )(y, var, noise)


def body(counts, topic_means, doc_topics_init, dirichlet_prior, chain_var, obs_noise):
    x = topic_means[0]
    y, xl, c = lax.axis_index("y"), lax.axis_index("xl"), lax.axis_index("c")
    chips = jnp.stack([lax.rem(y + dy, 4) * 2 + lax.rem(xl + dx, 2) for dy, dx in REL])
    counts = counts[0]
    init = doc_topics_init[0]

    b, b0, b1, level = slab_softmax(x)
    bx = xswap(b)
    u0, u1 = yfrom(b0, 3), yfrom(b1, 3)
    d0, d1 = yfrom(b0, 1), yfrom(b1, 1)
    other_init = across(init)
    theirs = across(counts)

    row = lax.broadcasted_iota(jnp.int32, (8, K), 0)
    pair = jnp.where(row % 2 == 0, level, jnp.logaddexp(level, across(level)))
    far = xswap(pair)
    levels = [jnp.where(row < 4, pair, far)]
    levels += [yfrom(levels[0], dy) for dy in (1, 2, 3)]

    x31, u20, d20 = xswap(u0), yfrom(u0, 3), yfrom(d1, 1)
    u31, d11 = yfrom(bx[HALF:], 3), yfrom(bx[HALF:], 1)
    x11 = xswap(d0)
    x21, u21 = xswap(u20), yfrom(u31, 3)

    index = {r: i for i, r in enumerate(REL)}
    orders = [[(0, 0), (0, 1), (3, 0), (1, 0)], [(2, 0), (3, 1), (1, 1)], [(2, 1)]]
    pieces = [(b, bx, u0, u1, d0, d1), (u20, d20, x31, u31, x11, d11), (x21, u21)]
    places = [
        [((0, 0), (0, HALF)), ((1, 0), (1, HALF)), ((2, 0), (3, 0)), ((4, 0), (5, 0))],
        [((0, 0), (1, 0)), ((2, 0), (3, 0)), ((4, 0), (5, 0))],
        [((0, 0), (1, 0))],
    ]
    slabs = tuple(tuple(index[r] for r in order) for order in orders)
    fetches = (slabs[0], slabs[1] + slabs[2], ())
    stay = lambda a: pltpu.with_memory_space_constraint(a, pltpu.HBM)
    heads = (stay(init), stay(other_init), *levels)
    given = (2 * chips + c, stay(counts), stay(theirs))
    bs, cs, parts = [], [], []
    for g in range(3):
        outs = first_sweep(
            slabs[g], fetches[g], places[g], heads, cs[1:] if g == 2 else given, pieces[g]
        )
        if g == 0:
            p, scale, whole, *outs = outs
            heads = (p, scale)
        parts.append(outs[0])
        bs.append(outs[1])
        cs.append(outs[2] if g < 2 else cs[1])
    part = parts[0] + parts[1] + parts[2]

    prior = dirichlet_prior[None, :]
    held = {(2, 1): (2, 0, HELD)}
    held.update({r: (g, i, i) for g in range(2) for i, r in enumerate(orders[g])})

    def swept(heads, wanted, stats=""):
        groups = sorted({held[r][0] for r in wanted}, reverse=True)
        slabs = tuple(
            tuple((index[r],) + held[r][1:] for r in wanted if held[r][0] == g) for g in groups
        )
        return sweep(heads, scale, slabs, [bs[g] for g in groups], [cs[g] for g in groups], stats)

    for _ in range(ITERS_E - 2):
        p, part = swept((part, across(part), p, prior), REL)

    stats = {}
    parts = []
    heads = (part, across(part), p, prior)
    for name, wanted in (
        ("stats_a", [(2, 1)]),
        ("stats_b", [(2, 0), (3, 1), (1, 1), (3, 0)]),
        ("stats_c", [(0, 0), (0, 1), (1, 0)]),
    ):
        outs = swept(heads, wanted, name)
        if not parts:
            p, *outs = outs
            heads = (p,)
        parts.append(outs[0])
        for j, r in enumerate(wanted):
            stats[r + (0,)], stats[r + (1,)] = outs[1 + 2 * j], outs[2 + 2 * j]
    part = parts[0] + parts[1] + parts[2]
    half0, half1 = scatter(stats)

    got = across(part)
    update = p.astype(F32) * (part + jnp.concatenate([got[DOCS:], got[:DOCS]], axis=0))
    concentration = prior + update[:DOCS]
    total = jnp.broadcast_to(jnp.sum(update, axis=0, keepdims=True), (8, K))
    total = total + xswap(total)
    total = total + yfrom(total, 3)
    total = total + yfrom(total, 2)

    rows = pseudo_rows(half0, half1, x, whole, total)
    rows = lax.all_to_all(rows, TM, 0, 0)
    smoothed = smooth(rows, chain_var[None, :], obs_noise[None, :])
    smoothed = lax.all_to_all(smoothed, TM, 0, 0)
    return smoothed.reshape(1, SLAB, K).astype(F32), concentration[None]


def solution(mesh):
    split = Mesh(mesh.devices.reshape(4, 2, 4, 2, 2), ("z", "xh", "y", "xl", "c"))
    docs = ("y", "xl", "c")
    placed = (P(TM, docs, None), P(TM, docs, None), P(TM, docs, None), P(), P(), P())

    return jax.shard_map(
        body,
        mesh=split,
        in_specs=placed,
        out_specs=(P(TM, docs, None), P(TM, docs, None)),
        check_vma=False,
    )
```
